256 devices in a mesh: dp: 32 (over z, y), fsdp: 8 (over x, core).
Axes of the slice: x: 4, y: 4, z: 8, core: 2. Of those that a mesh axis runs over, the one named last changes fastest.
Arguments:
- waveform: bfloat16 [8, 960, 1280], P('fsdp', 'dp'), may hold values from -6 to 6
- clip_lengths: int32 [8, 32, 1], replicated, may hold values from 320 to 38400, as said below
- conv_first: bfloat16 [10, 512], replicated, may hold values from -2 to 2
- conv_mid: bfloat16 [4, 3, 512, 512], replicated, may hold values from -0.15625 to 0.15625
- conv_last: bfloat16 [2, 2, 512, 512], replicated, may hold values from -0.1875 to 0.1875
- conv_gain: float32 [7, 512], replicated, may hold values from 0.1 to 1.9
- conv_shift: float32 [7, 512], replicated, may hold values from -1.5 to 1.5
- proj_gain: float32 [512], replicated, may hold values from 0.1 to 1.9
- proj_shift: float32 [512], replicated, may hold values from -1.5 to 1.5
- proj_weight: bfloat16 [512, 1280], replicated, may hold values from -0.25 to 0.25
- proj_bias: float32 [1280], replicated, may hold values from -1.5 to 1.5
- pos_weight: bfloat16 [16, 128, 80, 80], P('fsdp'), may hold values from -0.0625 to 0.0625
- pos_bias: float32 [1280], replicated, may hold values from -1.5 to 1.5
Outputs:
- features: bfloat16 [8, 2048, 1280], P('fsdp', 'dp')
The draws below stay inside these ranges and needn't reach their ends.
Inputs may be any that keep to these rules, and one draw needn't show every extreme that they name: `clip_lengths`: every length is a positive multiple of 320. The lengths of one source sum to 1280 times a whole number of blocks, at most 30; the block counts of one clip batch total 32 * 16, and in every clip batch some source holds exactly 30 blocks.
All inputs are finite; a program needn't handle non-finite values.
Results may differ from the reference program's by a relative error of at most 0.015.
Values may be sent and summed in bfloat16 or wider, within the bound.
A program may use at most 192 MiB of HBM per device.

```python
import jax
import jax.numpy as jnp
from jax import lax

C = 512
D = 1280
GROUPS = 16
TAPS = 128
FPB = 4
CLIPS = 1
NB = 16
CAP = 30
BLOCK = 1280
COLS = 8
N_DP = 32


def draw_clip_lengths(key, part):
    key_loads, key_order, key_cuts = jax.random.split(key, 3)
    group_count = N_DP // 8
    swings = jax.random.randint(key_loads, (COLS, group_count), 0, 3).astype(jnp.int32)
    swings = swings.at[:, 0].set(2)
    step_size = NB // 16
    pattern = jnp.array([7, -1, -1, -1, -1, -1, -1, -1], jnp.int32)
    ordered = NB + (swings[:, :, None] * step_size * pattern[None, None, :]).reshape(COLS, N_DP)
    orders = jax.vmap(lambda sub_key: jax.random.permutation(sub_key, N_DP))(jax.random.split(key_order, COLS)).astype(jnp.int32)
    column_ids = jnp.arange(COLS, dtype=jnp.int32)[:, None]
    block_counts = jnp.zeros((COLS, N_DP), jnp.int32).at[column_ids, orders].set(ordered)
    frame_counts = block_counts * FPB
    jitter_span = frame_counts // (4 * CLIPS)
    raw_bits = jax.random.randint(key_cuts, (COLS, N_DP, CLIPS - 1), 0, 1 << 20).astype(jnp.int32)
    jitter = raw_bits % (2 * jitter_span[:, :, None] + 1) - jitter_span[:, :, None]
    marks = jnp.arange(1, CLIPS, dtype=jnp.int32)[None, None, :] * frame_counts[:, :, None] // CLIPS + jitter
    bounds = jnp.concatenate([jnp.zeros((COLS, N_DP, 1), jnp.int32), marks, frame_counts[:, :, None]], axis=2)
    return ((bounds[:, :, 1:] - bounds[:, :, :-1]) * 320).astype(jnp.int32)


def block_levels(own_key, dims, shards, low, high):
    loudness = 1.0
    for dim, blocks in shards:
        steps = jax.random.uniform(jax.random.fold_in(jax.random.fold_in(own_key, 6), dim), (blocks,), jnp.float32, low / len(shards), high / len(shards))
        loudness = loudness * jnp.repeat(jnp.exp(steps), dims[dim] // blocks).reshape((-1,) + (1,) * (len(dims) - 1 - dim))
    return loudness


def centred(stream_key, shape, deviation, limit, cuts=(), held_as=jnp.bfloat16):
    values = deviation * jax.random.normal(stream_key, shape, jnp.float32)
    if cuts:
        values = values * block_levels(stream_key, shape, cuts, -0.22, 0.18)
    return jnp.clip(values, -limit, limit).astype(held_as)


def setup_inputs(seed: int = 0) -> dict:
    keys = jax.random.split(jax.random.key(seed), 14)
    waveform = centred(keys[0], (COLS, N_DP * CAP, BLOCK), 1.0, 6.0, ((0, 8), (1, 32)))
    clip_lengths = draw_clip_lengths(jax.random.fold_in(keys[13], 71), 0)
    conv_first = centred(keys[2], (10, C), 10 ** -0.5, 2.0)
    conv_mid = centred(keys[3], (4, 3, C, C), (3 * C) ** -0.5, 0.15625)
    conv_last = centred(keys[4], (2, 2, C, C), (2 * C) ** -0.5, 0.1875)
    conv_gain = jnp.clip(1.0 + 0.18 * jax.random.normal(keys[5], (7, C), jnp.float32), 0.1, 1.9)
    conv_shift = centred(keys[6], (7, C), 0.3, 1.5, (), jnp.float32)
    proj_gain = jnp.clip(1.0 + 0.18 * jax.random.normal(keys[7], (C,), jnp.float32), 0.1, 1.9)
    proj_shift = centred(keys[8], (C,), 0.3, 1.5, (), jnp.float32)
    proj_weight = centred(keys[9], (C, D), C ** -0.5, 0.25)
    proj_bias = centred(keys[10], (D,), 0.3, 1.5, (), jnp.float32)
    pos_weight = centred(keys[11], (GROUPS, TAPS, D // GROUPS, D // GROUPS), (TAPS * D // GROUPS) ** -0.5, 0.0625, ((0, 8),))
    pos_bias = centred(keys[12], (D,), 0.3, 1.5, (), jnp.float32)
    return dict(waveform=waveform, clip_lengths=clip_lengths, conv_first=conv_first, conv_mid=conv_mid, conv_last=conv_last, conv_gain=conv_gain, conv_shift=conv_shift, proj_gain=proj_gain, proj_shift=proj_shift, proj_weight=proj_weight, proj_bias=proj_bias, pos_weight=pos_weight, pos_bias=pos_bias)


NORM_EPS = 1e-05

def norm_gelu(summed, norm_gain, norm_shift):
    average = lax.optimization_barrier(jnp.mean(summed, axis=-1, keepdims=True))
    centered = summed - average
    spread = lax.optimization_barrier(jnp.mean(centered * centered, axis=-1, keepdims=True))
    normed = centered * lax.rsqrt(spread + NORM_EPS) * norm_gain + norm_shift
    return jax.nn.gelu(normed, approximate=False).astype(jnp.bfloat16)

def conv_stack(samples, conv_first, conv_mid, conv_last, conv_gain, conv_shift):
    batch_size, sample_count = samples.shape
    first_len = (sample_count - 10) // 5 + 1
    pieces = samples[:, :(first_len + 1) * 5].reshape(batch_size, first_len + 1, 5)
    window = jnp.concatenate([pieces[:, :-1], pieces[:, 1:]], axis=2)
    summed = jnp.einsum('blk,kc->blc', window.astype(jnp.float32), conv_first.astype(jnp.float32))
    hidden = norm_gelu(summed, conv_gain[0], conv_shift[0])
    for layer_index in range(6):
        if layer_index < 4:
            kernel, weight = (3, conv_mid[layer_index])
        else:
            kernel, weight = (2, conv_last[layer_index - 4])
        length = hidden.shape[1]
        out_len = (length - kernel) // 2 + 1
        summed = jnp.zeros((batch_size, out_len, weight.shape[2]), jnp.float32)
        for offset in range(kernel):
            strided = hidden[:, offset:offset + 2 * out_len - 1:2]
            summed = summed + jnp.einsum('blc,cd->bld', strided.astype(jnp.float32), weight[offset].astype(jnp.float32))
        hidden = norm_gelu(summed, conv_gain[layer_index + 1], conv_shift[layer_index + 1])
    return hidden

def project(frames, proj_gain, proj_shift, proj_weight, proj_bias):
    values = frames.astype(jnp.float32)
    average = lax.optimization_barrier(jnp.mean(values, axis=-1, keepdims=True))
    centered = values - average
    spread = lax.optimization_barrier(jnp.mean(centered * centered, axis=-1, keepdims=True))
    normed = (centered * lax.rsqrt(spread + NORM_EPS) * proj_gain + proj_shift).astype(jnp.bfloat16)
    return (jnp.dot(normed, proj_weight, preferred_element_type=jnp.float32) + proj_bias).astype(jnp.bfloat16)

def frame_segments(col_lengths, frame_ids):
    clip_ends = jnp.cumsum((col_lengths // 320).reshape(-1), dtype=jnp.int32)
    clip_index = lax.optimization_barrier(jnp.sum((clip_ends[None, :] <= frame_ids[:, None]).astype(jnp.int32), axis=1, dtype=jnp.int32))
    marker = jnp.arange(clip_ends.shape[0], dtype=jnp.int32)
    end_frame = lax.optimization_barrier(jnp.sum(jnp.where(marker[None, :] == clip_index[:, None], clip_ends[None, :], 0), axis=1, dtype=jnp.int32))
    usable = (frame_ids >= 0) & (frame_ids + 1 < end_frame)
    return (clip_index, usable)

def windows(extended, clip_index, usable, out_rows):
    rows_used = jnp.arange(out_rows, dtype=jnp.int32)[:, None] + jnp.arange(TAPS, dtype=jnp.int32)[None, :]
    centre = clip_index[TAPS // 2:TAPS // 2 + out_rows]
    same_clip = (clip_index[rows_used] == centre[:, None]) & usable[rows_used]
    picked = extended[rows_used]
    return jnp.where(same_clip[:, :, None], picked, jnp.zeros((), picked.dtype))

def finish(summed, bias_part, own_rows, usable_centre):
    total = own_rows.astype(jnp.float32) + jax.nn.gelu(summed + bias_part, approximate=False)
    return jnp.where(usable_centre[:, None], total, jnp.zeros((), jnp.float32)).astype(jnp.bfloat16)

def reference(waveform, clip_lengths, conv_first, conv_mid, conv_last, conv_gain, conv_shift, proj_gain, proj_shift, proj_weight, proj_bias, pos_weight, pos_bias):
    group_width = D // GROUPS
    block_frames = NB * FPB

    def one_column(column_data):
        wave_col, col_lengths = column_data
        block_counts = lax.optimization_barrier(jnp.sum(col_lengths, axis=1, dtype=jnp.int32)) // (FPB * 320)
        starts = jnp.cumsum(block_counts, dtype=jnp.int32) - block_counts
        block_ids = jnp.arange(N_DP * NB, dtype=jnp.int32)
        source = lax.optimization_barrier(jnp.sum((starts[None, :] <= block_ids[:, None]).astype(jnp.int32), axis=1, dtype=jnp.int32)) - 1
        source_ids = jnp.arange(N_DP, dtype=jnp.int32)
        start_of = lax.optimization_barrier(jnp.sum(jnp.where(source_ids[None, :] == source[:, None], starts[None, :], 0), axis=1, dtype=jnp.int32))
        row_ids = (source * CAP + block_ids - start_of).astype(jnp.int32)
        joined = jnp.take(wave_col, row_ids, axis=0).reshape(1, -1)
        joined = jnp.concatenate([joined, jnp.zeros((1, 80), joined.dtype)], axis=1)
        frames = conv_stack(joined, conv_first, conv_mid, conv_last, conv_gain, conv_shift)[0]
        projected = project(frames, proj_gain, proj_shift, proj_weight, proj_bias)
        half = TAPS // 2
        padded = jnp.concatenate([jnp.zeros((half, D), projected.dtype), projected, jnp.zeros((half, D), projected.dtype)], axis=0)
        frame_ids = jnp.arange(-half, N_DP * block_frames + half, dtype=jnp.int32)
        clip_index, usable = frame_segments(col_lengths, frame_ids)

        def one_block(block_index):
            first = (block_index * block_frames).astype(jnp.int32)
            extended = lax.dynamic_slice_in_dim(padded, first, block_frames + TAPS, 0)
            ids_here = lax.dynamic_slice_in_dim(clip_index, first, block_frames + TAPS, 0)
            usable_here = lax.dynamic_slice_in_dim(usable, first, block_frames + TAPS, 0)
            picked = windows(extended, ids_here, usable_here, block_frames).reshape(block_frames, TAPS, GROUPS, group_width)
            summed = jnp.einsum('otgi,gtin->ogn', picked.astype(jnp.float32), pos_weight.astype(jnp.float32)).reshape(block_frames, D)
            return finish(summed, pos_bias, extended[half:half + block_frames], usable_here[half:half + block_frames])
        result = lax.map(one_block, jnp.arange(N_DP, dtype=jnp.int32))
        return result.reshape(N_DP * block_frames, D)
    return lax.map(one_column, (waveform, clip_lengths))
```

```python
import jax
import jax.numpy as jnp
from jax import lax
from jax.sharding import PartitionSpec as P
from jax.experimental import pallas as pl
from jax.experimental.pallas import tpu as pltpu

NORM_EPS = 1e-5
R2 = 0.7071067811865476

TAPS = 128
FPB = 4
NB = 16


def padded_2(value, sides, width):
    for axis, dim in sides:
        size, length = (lax.axis_size(axis), value.shape[dim])
        up = [(i, (i + 1) % size) for i in range(size - 1)]
        down = [(j, i) for i, j in up]
        last = lax.slice_in_dim(value, length - width, length, axis=dim)
        leading = lax.slice_in_dim(value, 0, width, axis=dim)
        before = lax.ppermute(last, axis, up)
        after = lax.ppermute(leading, axis, down)
        value = jnp.concatenate([before, value, after], axis=dim)
    return value


def norm_act(h, gain, shift):
    mean = jnp.sum(h, axis=-1, keepdims=True) * (1.0 / h.shape[-1])
    cen = h - mean
    var = jnp.sum(cen * cen, axis=-1, keepdims=True) * (1.0 / h.shape[-1])
    z = cen * lax.rsqrt(var + NORM_EPS) * gain + shift
    return (z * R2) * (1.0 + lax.erf(z))

def conv_kernel(xt_ref, xh_ref, w0_ref, gain_ref, shift_ref, pg_ref, ps_ref, pb_ref, wm_hbm, wl_hbm, wp_hbm,
                out_ref, a0, a1, a2, a3, a4, a5, hal, wm, wl, wp, sems):
    copies = [pltpu.make_async_copy(wm_hbm.at[i], wm.at[i], sems.at[i]) for i in range(4)]
    copies += [pltpu.make_async_copy(wl_hbm.at[i], wl.at[i], sems.at[4 + i]) for i in range(2)]
    copies += [pltpu.make_async_copy(wp_hbm, wp, sems.at[6])]
    for c in copies:
        c.start()
    f32, bf = jnp.float32, jnp.bfloat16
    dn = (((0,), (0,)), ((), ()))
    g0, s0 = gain_ref[0:1, :], shift_ref[0:1, :]
    w0 = w0_ref[...]

    def put(li, rows):
        for t in range(4):
            hal[li, t, 0:rows.shape[0], :] = rows[:, 128 * t:128 * t + 128]

    def pick(li, start, size, stride=1):
        ds = pl.ds(start, size, stride=stride) if stride > 1 else pl.ds(start, size)
        return jnp.concatenate([hal[li, t, ds, :] for t in range(4)], axis=1)
    h = lax.dot_general(xh_ref[...].astype(bf), w0, (((1,), (0,)), ((), ())), preferred_element_type=f32)
    put(0, norm_act(h, g0, s0))

    def l0(i, c):
        for q in range(2):
            p = 2 * i + q
            win = xt_ref[pl.ds(5 * p, 16), :].astype(bf)
            h = lax.dot_general(win, w0, dn, preferred_element_type=f32)
            a = norm_act(h, g0, s0).astype(bf)
            a0[p] = a[0:64]
            a0[p + 32] = a[64:128]
        return c
    lax.fori_loop(0, 16, l0, 0)

    srcs = [a0, a1, a2, a3, a4, a5]
    counts = [32, 16, 8, 4, 2, 1]
    for L in range(1, 7):
        src = srcs[L - 1]
        n = counts[L - 1]
        K = 3 if L <= 4 else 2
        copies[L - 1].wait()
        w = (lambda k, L=L: wm[L - 1, k]) if L <= 4 else (lambda k, L=L: wl[L - 5, k])
        g, s = gain_ref[L:L + 1, :], shift_ref[L:L + 1, :]
        G = min(4, n)
        if K == 3:
            up = jnp.concatenate([src[0].astype(f32)[1:64], pick(L - 1, 0, 1)], axis=0)
            src[2 * n] = up.astype(bf)
        def body(i, c, src=src, n=n, K=K, G=G, w=w, g=g, s=s, L=L, halo=False):
            acc = None
            for k in range(K):
                lhs = [src[2 * (G * i + q) + k] for q in range(G)]
                if halo:
                    lhs.append(jnp.concatenate([pick(L - 1, k, 8, 2), jnp.zeros((8, 512), f32)], axis=0).astype(bf))
                lhs = jnp.concatenate(lhs, axis=0) if len(lhs) > 1 else lhs[0]
                d = jnp.dot(lhs, w(k), preferred_element_type=f32)
                acc = d if acc is None else acc + d
            a = norm_act(acc, g, s)
            if halo:
                put(L, a[64 * G:64 * G + 8])
            if L < 6:
                dst = srcs[L]
                for q in range(G):
                    dst[G * i + q] = a[64 * q:64 * q + 64].astype(bf)
                return c
            return a
        r = body(0, 0, halo=(L <= 3))
        if n // G > 1:
            lax.fori_loop(1, n // G, body, 0)
    v = r.astype(bf).astype(f32)
    mean = jnp.sum(v, axis=-1, keepdims=True) * (1.0 / 512)
    cen = v - mean
    var = jnp.sum(cen * cen, axis=-1, keepdims=True) * (1.0 / 512)
    nf = (cen * lax.rsqrt(var + NORM_EPS) * pg_ref[...] + ps_ref[...]).astype(bf)
    copies[6].wait()
    out_ref[...] = (jnp.dot(nf, wp[...], preferred_element_type=f32) + pb_ref[...]).astype(bf)


def conv_stack_call(xt, xh, conv_first, conv_mid, conv_last, conv_gain, conv_shift, proj_gain, proj_shift, proj_weight, proj_bias):
    w0 = jnp.concatenate([conv_first, jnp.zeros((6, 512), conv_first.dtype)], axis=0)
    V = pl.BlockSpec(memory_space=pltpu.VMEM)
    A = pl.BlockSpec(memory_space=pl.ANY)
    bf = jnp.bfloat16
    return pl.pallas_call(
        conv_kernel,
        out_shape=jax.ShapeDtypeStruct((64, 1280), bf),
        in_specs=[V] * 8 + [A] * 3,
        out_specs=V,
        scratch_shapes=[pltpu.VMEM((65, 64, 512), bf), pltpu.VMEM((33, 64, 512), bf), pltpu.VMEM((17, 64, 512), bf),
                        pltpu.VMEM((9, 64, 512), bf), pltpu.VMEM((4, 64, 512), bf), pltpu.VMEM((2, 64, 512), bf),
                        pltpu.VMEM((4, 4, 24, 128), jnp.float32),
                        pltpu.VMEM((4, 3, 512, 512), bf), pltpu.VMEM((2, 2, 512, 512), bf), pltpu.VMEM((512, 1280), bf),
                        pltpu.SemaphoreType.DMA((7,))],
        compiler_params=pltpu.CompilerParams(vmem_limit_bytes=50 << 20),
        name="conv_stack",
    )(xt, xh, w0, conv_gain * R2, conv_shift * R2, proj_gain[None], proj_shift[None], proj_bias[None], conv_mid, conv_last, proj_weight)


def prep_samples(own, nxt):
    fr = own.reshape(64, 320).astype(jnp.float32)
    nx = nxt.astype(jnp.float32)
    tail = jnp.concatenate([fr[1:, :16], nx[None, :16]], axis=0)
    S = jnp.concatenate([fr, tail], axis=1)
    xt = jnp.concatenate([S[:, :176], S[:, 160:336]], axis=0).T
    idx = nx[:80].reshape(16, 5)
    nxt_idx = jnp.concatenate([idx[1:], jnp.zeros((1, 5), jnp.float32)], axis=0)
    xh = jnp.concatenate([idx, nxt_idx, jnp.zeros((16, 6), jnp.float32)], axis=1)
    return xt, xh

WROWS = 133 * 80 + 16

def pos_kernel(src_ref, wb_hbm, bias_ref, out_ref, x3, cc, wb, sems):
    f32, bf = jnp.float32, jnp.bfloat16
    copies = [pltpu.make_async_copy(wb_hbm.at[g], wb.at[g], sems.at[g]) for g in range(2)]
    for c in copies:
        c.start()
    lane = lax.broadcasted_iota(jnp.int32, (96 * 8, 128), 1)
    cc[...] = jnp.concatenate([src_ref[2, 64:128].reshape(32, 2, 8, 128)[:, 0].reshape(256, 128)] * 2, axis=1).astype(bf)
    for a in range(3):
        full = src_ref[a].reshape(97, 2, 8, 128)
        ev, od = full[:, 0].reshape(97 * 8, 128), full[:, 1].reshape(97 * 8, 128)
        for par in range(2):
            f0 = (ev if par == 0 else od)[0:768]
            f1 = od[0:768] if par == 0 else ev[8:776]
            f2 = (ev if par == 0 else od)[8:776]
            r1 = pltpu.roll(f1, 80, 1)
            r2 = pltpu.roll(f2, 32, 1)
            v0 = jnp.where(lane < 80, f0, r1)
            v1 = jnp.where(lane < 32, r1, jnp.where(lane < 112, r2, 0.0))
            v = jnp.concatenate([v0, v1], axis=1)
            x3[a, par, 0] = v.astype(bf)
            x3[a, par, 1, 0:752, :] = v[8:760].astype(bf)
    for c in copies:
        c.wait()
    plan = ((0, 0, 0), (1, 1, 0), (0, 1, 16), (1, 0, 32))

    def body(i, acc):
        ctr = cc[...]
        masks = []
        for par, al, off in plan:
            masks.append(x3[2, par, al, pl.ds(pl.multiple_of(48 * i, 16) + off, 256), :] == ctr)
        out = []
        for g in range(2):
            lhs = jnp.concatenate([
                jnp.where(m, x3[g, par, al, pl.ds(pl.multiple_of(48 * i, 16) + off, 256), :], jnp.zeros((), bf))
                for m, (par, al, off) in zip(masks, plan)], axis=1)
            rhs = jnp.concatenate([
                jnp.concatenate([wb[g, pl.ds(pl.multiple_of(960 * i, 16) + 240 * s + 80, 256), :],
                                 wb[g, pl.ds(pl.multiple_of(960 * i, 16) + 240 * s, 256), :]], axis=1)
                for s in range(4)], axis=0)
            out.append(acc[g] + jnp.dot(lhs, rhs, preferred_element_type=f32))
        return tuple(out)
    acc = lax.fori_loop(0, 11, body, (jnp.zeros((256, 256), f32),) * 2)
    for g in range(2):
        halves = []
        for v in range(2):
            pos = acc[g][:, 128 * v:128 * v + 128] + bias_ref[g]
            own = src_ref[g, 64:128].reshape(32, 2, 8, 128)[:, v].reshape(256, 128)
            cid = src_ref[2, 64:128].reshape(32, 2, 8, 128)[:, v].reshape(256, 128)
            gel = 0.5 * pos * (1.0 + lax.erf(pos * 0.7071067811865476))
            res = jnp.where(cid >= 0.0, own + gel, 0.0)
            halves.append(res.reshape(32, 1, 8, 128))
        out_ref[g] = jnp.concatenate(halves, axis=1).reshape(64, 8, 128)

def pos_call(src, wb, bias):
    V = pl.BlockSpec(memory_space=pltpu.VMEM)
    A = pl.BlockSpec(memory_space=pl.ANY)
    bf = jnp.bfloat16
    return pl.pallas_call(
        pos_kernel,
        out_shape=jax.ShapeDtypeStruct((2, 64, 8, 128), jnp.float32),
        in_specs=[V, A, V], out_specs=V,
        scratch_shapes=[pltpu.VMEM((3, 2, 2, 768, 256), bf), pltpu.VMEM((256, 256), bf), pltpu.VMEM((2, WROWS, 128), bf),
                        pltpu.SemaphoreType.DMA((2,))],
        compiler_params=pltpu.CompilerParams(vmem_limit_bytes=50 << 20),
        name="pos_conv",
    )(src, wb, bias)

def pad_weights(w):
    w = w.reshape(2, 128 * 80, 80)
    return jnp.pad(w, ((0, 0), (80, WROWS - 80 - 10240), (0, 48)))


def frame_segments(col_lengths, frame_ids):
    clip_ends = jnp.cumsum((col_lengths // 320).reshape(-1), dtype=jnp.int32)
    clip_index = jnp.sum(
        (clip_ends[None, :] <= frame_ids[:, None]).astype(jnp.int32), axis=1, dtype=jnp.int32
    )
    marker = jnp.arange(clip_ends.shape[0], dtype=jnp.int32)
    end_frame = jnp.sum(
        jnp.where(marker[None, :] == clip_index[:, None], clip_ends[None, :], 0),
        axis=1,
        dtype=jnp.int32,
    )
    usable = (frame_ids >= 0) & (frame_ids + 1 < end_frame)
    return (clip_index, usable)


def per_device(
    waveform,
    clip_lengths,
    conv_first,
    conv_mid,
    conv_last,
    conv_gain,
    conv_shift,
    proj_gain,
    proj_shift,
    proj_weight,
    proj_bias,
    pos_weight,
    pos_bias,
):
    dp_size = lax.axis_size("dp")
    fs_size = lax.axis_size("fsdp")
    my_rank = lax.axis_index("dp")
    column = lax.axis_index("fsdp")
    capacity = waveform.shape[1]
    block_len = waveform.shape[2]
    send_slots = (capacity + dp_size - 1) // dp_size
    half = TAPS // 2
    frame_rows = NB * FPB
    col_lengths = lax.dynamic_index_in_dim(clip_lengths, column, 0, keepdims=False)
    block_counts = jnp.sum(col_lengths, axis=1, dtype=jnp.int32) // block_len
    starts = jnp.cumsum(block_counts, dtype=jnp.int32) - block_counts
    sources = jnp.arange(dp_size, dtype=jnp.int32)
    my_start = starts[my_rank]
    my_blocks = waveform[0]
    tail_part = jnp.concatenate([my_blocks[1:, :128], jnp.zeros((1, 128), my_blocks.dtype)], axis=0)
    strips = jnp.concatenate([my_blocks, tail_part], axis=1)
    width = strips.shape[1]
    padded = jnp.concatenate(
        [strips, jnp.zeros((send_slots * dp_size - capacity, width), strips.dtype)], axis=0
    )
    received = lax.all_to_all(
        jnp.roll(padded.reshape(send_slots, dp_size, width), my_start % dp_size, axis=1),
        "dp",
        split_axis=1,
        concat_axis=0,
        tiled=True,
    )
    item_index = jnp.arange(send_slots, dtype=jnp.int32)
    local_pos = item_index[None, :] * dp_size + (my_rank - starts[:, None]) % dp_size
    live = local_pos < block_counts[:, None]
    target = (starts[:, None] + local_pos) // dp_size
    chooser = (
        target.reshape(-1)[None, :] == jnp.arange(NB, dtype=jnp.int32)[:, None]
    ) & live.reshape(-1)[None, :]
    flat_rows = received.reshape(dp_size * send_slots, -1)
    arrived = jnp.dot(
        chooser.astype(flat_rows.dtype), flat_rows, preferred_element_type=jnp.float32
    ).astype(flat_rows.dtype)
    slots_back = (NB + dp_size - 1) // dp_size
    item_index = jnp.arange(slots_back, dtype=jnp.int32)
    slot_ids = jnp.arange(NB, dtype=jnp.int32)

    def first_slot(target_rank, source_rank):
        return jnp.maximum((target_rank * NB - source_rank + dp_size - 1) // dp_size, 0)

    targets = jnp.arange(dp_size, dtype=jnp.int32)
    slot_index = first_slot(targets, my_rank)[:, None] + item_index[None, :]
    usable_out = (slot_index < NB) & ((my_rank + slot_index * dp_size) // NB == targets[:, None])
    picker = (slot_index.reshape(-1)[:, None] == slot_ids[None, :]) & usable_out.reshape(-1)[
        :, None
    ]
    sending = jnp.dot(
        picker.astype(arrived.dtype), arrived, preferred_element_type=jnp.float32
    ).astype(arrived.dtype)
    returned = lax.all_to_all(
        sending.reshape(dp_size, slots_back, -1), "dp", split_axis=0, concat_axis=0, tiled=True
    )
    slot_in = first_slot(my_rank, sources)[:, None] + item_index[None, :]
    usable_in = (slot_in < NB) & ((sources[:, None] + slot_in * dp_size) // NB == my_rank)
    position = sources[:, None] + slot_in * dp_size - my_rank * NB
    placer = (position.reshape(-1)[None, :] == slot_ids[:, None]) & usable_in.reshape(-1)[None, :]
    ordered = jnp.dot(
        placer.astype(returned.dtype),
        returned.reshape(dp_size * slots_back, -1),
        preferred_element_type=jnp.float32,
    ).astype(returned.dtype)
    xt, xh = prep_samples(ordered[:, :block_len], ordered[NB - 1, block_len:])
    projected = conv_stack_call(
        xt, xh, conv_first, conv_mid, conv_last, conv_gain, conv_shift, proj_gain, proj_shift, proj_weight, proj_bias
    )
    group_here = pos_weight.shape[0]
    group_width = pos_weight.shape[2]
    width_here = group_here * group_width
    mine = lax.all_to_all(
        projected.reshape(1, frame_rows, fs_size, width_here), "fsdp", split_axis=2, concat_axis=0, tiled=True
    )[:, :, 0, :]
    extended = padded_2(mine, (("dp", 1),), half)
    frame_ids = my_rank * frame_rows - half + jnp.arange(frame_rows + TAPS, dtype=jnp.int32)
    clip_ids, usables = jax.vmap(lambda col: frame_segments(col, frame_ids))(clip_lengths)
    lanes = jnp.transpose(extended, (1, 0, 2)).reshape(frame_rows + TAPS, fs_size, group_here, group_width)
    lanes = jnp.pad(lanes.transpose(2, 0, 1, 3).astype(jnp.float32), ((0, 0), (0, 2), (0, 0), (0, 48)))
    marks = jnp.where(usables, clip_ids, -1).T.astype(jnp.float32)
    marks = jnp.pad(marks, ((0, 2), (0, 0)), constant_values=-1)
    marks = jnp.broadcast_to(marks[None, :, :, None], (1, frame_rows + TAPS + 2, fs_size, 128))
    bias_part = lax.dynamic_slice_in_dim(pos_bias, column * width_here, width_here, 0)
    bias_part = jnp.pad(bias_part.reshape(group_here, 1, group_width), ((0, 0), (0, 0), (0, 48)))
    finished = pos_call(jnp.concatenate([lanes, marks], axis=0), pad_weights(pos_weight), bias_part)
    finished = finished[..., :group_width].astype(jnp.bfloat16).transpose(2, 1, 0, 3)
    answered = lax.all_to_all(
        finished.reshape(fs_size, frame_rows, 1, width_here), "fsdp", split_axis=0, concat_axis=2, tiled=True
    )
    return answered.reshape(1, frame_rows, -1)


def solution(mesh):
    return jax.shard_map(
        per_device,
        mesh=mesh,
        in_specs=(
            P("fsdp", "dp", None),
            P(),
            P(),
            P(),
            P(),
            P(),
            P(),
            P(),
            P(),
            P(),
            P(),
            P("fsdp", None, None, None),
            P(),
        ),
        out_specs=P("fsdp", "dp", None),
        check_vma=False,
    )
```

```python
import jax
import jax.numpy as jnp
from jax import lax
from jax.experimental import pallas as pl
from jax.experimental.pallas import tpu as pltpu
from jax.sharding import PartitionSpec as P

NORM_EPS = 1e-5
R2 = 0.7071067811865476
F32, BF = jnp.float32, jnp.bfloat16
MESH = pl.DeviceIdType.MESH
NDP, NFS = 32, 8


def norm_act(h, gain, shift):
    mean = jnp.sum(h, axis=-1, keepdims=True) * (1.0 / h.shape[-1])
    cen = h - mean
    var = jnp.sum(cen * cen, axis=-1, keepdims=True) * (1.0 / h.shape[-1])
    z = cen * lax.rsqrt(var + NORM_EPS) * gain + shift
    return (z * R2) * (1.0 + lax.erf(z))


def encode_kernel(lens_ref, wave_ref, w0_ref, gain_ref, shift_ref, pg_ref, ps_ref, pb_ref, wm_hbm, wl_hbm, wp_hbm,
                  out_ref, blk, blkb, send1, recv1, send2, recv2, rows, xt, a0, a1, a2, a3, a4, a5, hal, fr, wm, wl, wp,
                  wsem, s1, r1, s2, r2):
    me, col = lax.axis_index("dp"), lax.axis_index("fsdp")
    barrier = pltpu.get_barrier_semaphore()
    for n in range(1, NDP):
        pl.semaphore_signal(barrier, inc=1, device_id={"dp": lax.rem(me + n, NDP)}, device_id_type=MESH)
    copies = [pltpu.make_async_copy(wm_hbm.at[i], wm.at[i], wsem.at[i]) for i in range(4)]
    copies += [pltpu.make_async_copy(wl_hbm.at[i], wl.at[i], wsem.at[4 + i]) for i in range(2)]
    copies += [pltpu.make_async_copy(wp_hbm, wp, wsem.at[6])]
    for c in copies:
        c.start()

    blk[...] = jnp.zeros((512, 128), F32)
    wave = wave_ref[0].astype(F32)
    for r in range(10):
        blk[pl.ds(r, 30, stride=16), :] = wave[:, 128 * r:128 * r + 128]
    blk[pl.ds(10, 29, stride=16), :] = wave[1:30, 0:128]
    blkb[...] = blk[...].astype(BF).reshape(32, 16, 128)

    def tally(s, carry):
        total, mine, owners = carry[0], carry[1], carry[2:]
        mine = jnp.where(s == me, total, mine)
        total = total + lens_ref[col, s]
        owners = tuple(o + jnp.where(total <= (me + NDP * j) * 1280, 1, 0) for j, o in enumerate(owners))
        return (total, mine) + owners
    zero = jnp.int32(0)
    res = lax.fori_loop(0, NDP, tally, (zero,) * 18)
    start, owners = res[1] // 1280, res[2:]

    for t in range(NDP):
        send1[t] = blkb[(t - start) & 31]
    recv1[me] = send1[me]
    pl.semaphore_wait(barrier, NDP - 1)
    first = []
    for n in range(1, NDP):
        to = lax.rem(me + n, NDP)
        c = pltpu.make_async_remote_copy(src_ref=send1.at[to], dst_ref=recv1.at[me], send_sem=s1.at[n],
                                         recv_sem=r1.at[n], device_id={"dp": to}, device_id_type=MESH)
        c.start()
        first.append(c)
    for c in first:
        c.wait()
    half, slot = me // 16, me % 16
    for j in range(16):
        send2[j] = recv1[jnp.minimum(owners[j], 31)]
    second = []
    for j in range(16):
        to = 2 * j + half
        c = pltpu.make_async_remote_copy(src_ref=send2.at[j], dst_ref=recv2.at[slot], send_sem=s2.at[j],
                                         recv_sem=r2.at[slot], device_id={"dp": to}, device_id_type=MESH)
        second.append((to, c))

        @pl.when(to != me)
        def _():
            c.start()

        @pl.when(to == me)
        def _():
            recv2[slot] = send2[j]
    odd = me % 2
    for i in range(16):
        c = pltpu.make_async_remote_copy(src_ref=send2.at[0], dst_ref=recv2.at[i], send_sem=s2.at[0],
                                         recv_sem=r2.at[i], device_id={"dp": me}, device_id_type=MESH)

        @pl.when(16 * odd + i != me)
        def _():
            c.wait_recv()
    for to, c in second:
        @pl.when(to != me)
        def _():
            c.wait_send()

    rows[...] = recv2[...].astype(F32).reshape(256, 128)
    flat = jnp.concatenate([rows[pl.ds(r, 16, stride=16), :] for r in range(11)], axis=1)
    y = jnp.concatenate([flat[:, 160 * e:160 * e + 256] for e in range(8)], axis=0)
    xt[...] = y.T
    halo = jnp.broadcast_to(rows[250:251, :], (16, 128))
    line = lax.broadcasted_iota(jnp.int32, (16, 128), 0)
    xh = halo
    for p in range(1, 15):
        xh = jnp.where(line == p, pltpu.roll(halo, 128 - 5 * p, 1), xh)

    dn = (((0,), (0,)), ((), ()))
    g0, b0 = gain_ref[0:1, :], shift_ref[0:1, :]
    w0 = w0_ref[...]

    def put(li, v):
        for t in range(4):
            hal[li, t, 0:v.shape[0], :] = v[:, 128 * t:128 * t + 128]

    def pick(li, begin, size, stride=1):
        ds = pl.ds(begin, size, stride=stride) if stride > 1 else pl.ds(begin, size)
        return jnp.concatenate([hal[li, t, ds, :] for t in range(4)], axis=1)

    h = jnp.dot(xh[:, 0:16].astype(BF), w0, preferred_element_type=F32)
    hal[...] = jnp.zeros(hal.shape, F32)
    put(0, norm_act(h, g0, b0))

    def l0(i, c):
        for q in range(2):
            p = 2 * i + q
            win = xt[pl.ds(5 * p, 16), :].astype(BF)
            h = lax.dot_general(win, w0, dn, preferred_element_type=F32)
            a = norm_act(h, g0, b0).astype(BF).reshape(4, 2, 16, 512)
            a0[p] = a[:, 0].reshape(64, 512)
            a0[p + 32] = a[:, 1].reshape(64, 512)
        return c
    lax.fori_loop(0, 16, l0, 0)

    srcs = [a0, a1, a2, a3, a4, a5]
    counts = [32, 16, 8, 4, 2, 1]
    for L in range(1, 7):
        src, n = srcs[L - 1], counts[L - 1]
        K = 3 if L <= 4 else 2
        G = min(4, n)
        copies[L - 1].wait()
        w = (lambda k, L=L: wm[L - 1, k]) if L <= 4 else (lambda k, L=L: wl[L - 5, k])
        g, s = gain_ref[L:L + 1, :], shift_ref[L:L + 1, :]
        if K == 3:
            v = src[0].astype(F32)
            src[2 * n] = jnp.concatenate([v[16:64], v[1:16], pick(L - 1, 0, 1)], axis=0).astype(BF)

        def body(i, c, src=src, K=K, G=G, w=w, g=g, s=s, L=L, halo=False):
            acc = None
            for k in range(K):
                lhs = [src[2 * (G * i + q) + k] for q in range(G)]
                if halo:
                    lhs.append(jnp.concatenate([pick(L - 1, k, 8, 2), jnp.zeros((8, 512), F32)], axis=0).astype(BF))
                lhs = jnp.concatenate(lhs, axis=0) if len(lhs) > 1 else lhs[0]
                d = jnp.dot(lhs, w(k), preferred_element_type=F32)
                acc = d if acc is None else acc + d
            a = norm_act(acc, g, s)
            if halo:
                put(L, a[64 * G:64 * G + 8])
            if L == 6:
                return a
            for q in range(G):
                srcs[L][G * i + q] = a[64 * q:64 * q + 64].astype(BF)
            return c
        last = body(0, 0, halo=(L <= 3))
        if n // G > 1:
            lax.fori_loop(1, n // G, body, 0)

    v = last.astype(BF).astype(F32)
    for t in range(4):
        for q in range(4):
            fr[t, pl.ds(q, 16, stride=4), :] = v[16 * q:16 * q + 16, 128 * t:128 * t + 128]
    v = jnp.concatenate([fr[t] for t in range(4)], axis=1)
    mean = jnp.sum(v, axis=-1, keepdims=True) * (1.0 / 512)
    cen = v - mean
    var = jnp.sum(cen * cen, axis=-1, keepdims=True) * (1.0 / 512)
    nf = (cen * lax.rsqrt(var + NORM_EPS) * pg_ref[...] + ps_ref[...]).astype(BF)
    copies[6].wait()
    pr = jnp.dot(nf, wp[...], preferred_element_type=F32) + pb_ref[...]
    gap = jnp.zeros((64, 48), F32)
    for q in range(8):
        parts = []
        for g in range(2):
            parts += [pr[:, 160 * q + 80 * g:160 * q + 80 * g + 80], gap]
        out_ref[q] = jnp.concatenate(parts, axis=1).astype(BF)


def encode_call(waveform, clip_lengths, conv_first, conv_mid, conv_last, conv_gain, conv_shift, proj_gain, proj_shift, proj_weight, proj_bias):
    w0 = jnp.concatenate([conv_first, jnp.zeros((6, 512), conv_first.dtype)], axis=0)
    V = pl.BlockSpec(memory_space=pltpu.VMEM)
    A = pl.BlockSpec(memory_space=pl.ANY)
    S = pl.BlockSpec(memory_space=pltpu.SMEM)
    D = pltpu.SemaphoreType.DMA
    return pl.pallas_call(
        encode_kernel,
        out_shape=jax.ShapeDtypeStruct((8, 64, 256), BF),
        in_specs=[S] + [V] * 7 + [A] * 3,
        out_specs=V,
        scratch_shapes=[pltpu.VMEM((512, 128), F32), pltpu.VMEM((32, 16, 128), BF), pltpu.VMEM((32, 16, 128), BF),
                        pltpu.VMEM((32, 16, 128), BF), pltpu.VMEM((16, 16, 128), BF), pltpu.VMEM((16, 16, 128), BF),
                        pltpu.VMEM((256, 128), F32), pltpu.VMEM((256, 128), F32),
                        pltpu.VMEM((65, 64, 512), BF), pltpu.VMEM((33, 64, 512), BF), pltpu.VMEM((17, 64, 512), BF),
                        pltpu.VMEM((9, 64, 512), BF), pltpu.VMEM((4, 64, 512), BF), pltpu.VMEM((2, 64, 512), BF),
                        pltpu.VMEM((4, 4, 24, 128), F32), pltpu.VMEM((4, 64, 128), F32),
                        pltpu.VMEM((4, 3, 512, 512), BF), pltpu.VMEM((2, 2, 512, 512), BF), pltpu.VMEM((512, 1280), BF),
                        D((7,)), D((32,)), D((32,)), D((16,)), D((16,))],
        compiler_params=pltpu.CompilerParams(vmem_limit_bytes=50 << 20, collective_id=0, has_side_effects=True),
        name="route_and_encode",
    )(clip_lengths[:, :, 0], waveform, w0, conv_gain * R2, conv_shift * R2, proj_gain[None], proj_shift[None], proj_bias[None], conv_mid, conv_last, proj_weight)


WROWS = 133 * 80 + 16
PLAN = ((0, 0, 0), (1, 1, 0), (0, 1, 16), (1, 0, 32))


def pos_kernel(slab_ref, lens_ref, bias_ref, wb_hbm, out_ref, rcv, src, x3, cc, wb, res, fin, ret, wsem, s1, r1, s2, r2):
    me, col = lax.axis_index("dp"), lax.axis_index("fsdp")
    barrier = pltpu.get_barrier_semaphore()
    peers = [(dr, dq) for dr in (0, 1, -1) for dq in range(NFS) if (dr, dq) != (0, 0)]

    def at(dr, dq):
        return {"dp": lax.rem(me + dr + NDP, NDP), "fsdp": lax.rem(col + dq + NFS, NFS)}
    for dr, dq in peers:
        pl.semaphore_signal(barrier, inc=1, device_id=at(dr, dq), device_id_type=MESH)
    weights = [pltpu.make_async_copy(wb_hbm.at[g], wb.at[g], wsem.at[g]) for g in range(2)]
    for c in weights:
        c.start()
    rcv[1, col] = slab_ref[col]
    pl.semaphore_wait(barrier, len(peers))
    sends = []
    for n, (dr, dq) in enumerate(peers):
        to = at(dr, dq)
        c = pltpu.make_async_remote_copy(src_ref=slab_ref.at[to["fsdp"]], dst_ref=rcv.at[1 - dr, col],
                                         send_sem=s1.at[n], recv_sem=r1.at[n], device_id=to, device_id_type=MESH)
        c.start()
        sends.append(c)

    row = lax.broadcasted_iota(jnp.int32, (128, 128), 0)
    lane = lax.broadcasted_iota(jnp.int32, (128, 128), 1)
    upper = jnp.where(row <= lane, 1.0, 0.0).astype(BF)
    ends = jnp.dot(lens_ref[...].astype(BF), upper, preferred_element_type=F32)
    ends = jnp.where(lax.broadcasted_iota(jnp.int32, (8, 128), 1) < NDP, ends, 1e9)
    frame = lax.broadcasted_iota(jnp.int32, (195, 8, 128), 0) + (64 * me - 64)
    past = jnp.where(ends[None] <= frame.astype(F32), 1.0, 0.0)
    clip = jnp.sum(past, axis=2, keepdims=True)
    here, after = clip[0:194], clip[1:195]
    ok = (here == after) & (frame[0:194, :, 0:1] >= 0) & (here < NDP)
    src[2, 0:1552, :] = jnp.broadcast_to(jnp.where(ok, here, -1.0), (194, 8, 128)).reshape(1552, 128)
    for c in sends:
        c.wait()

    for g in range(2):
        src[g, 1536:1552, :] = jnp.zeros((16, 128), F32)
        for part in range(3):
            for c in range(NFS):
                src[g, pl.ds(512 * part + c, 64, stride=8), :] = rcv[part, c, :, 128 * g:128 * g + 128].astype(F32)
    cc[...] = jnp.concatenate([src[2, 512:1024].reshape(32, 2, 8, 128)[:, 0].reshape(256, 128)] * 2, axis=1).astype(BF)
    lane = lax.broadcasted_iota(jnp.int32, (768, 128), 1)
    for a in range(3):
        full = src[a].reshape(97, 2, 8, 128)
        ev, od = full[:, 0].reshape(776, 128), full[:, 1].reshape(776, 128)
        for par in range(2):
            f0 = (ev if par == 0 else od)[0:768]
            f1 = od[0:768] if par == 0 else ev[8:776]
            f2 = (ev if par == 0 else od)[8:776]
            t1 = pltpu.roll(f1, 80, 1)
            t2 = pltpu.roll(f2, 32, 1)
            v0 = jnp.where(lane < 80, f0, t1)
            v1 = jnp.where(lane < 32, t1, jnp.where(lane < 112, t2, 0.0))
            v = jnp.concatenate([v0, v1], axis=1)
            x3[a, par, 0] = v.astype(BF)
            x3[a, par, 1, 0:752, :] = v[8:760].astype(BF)
    for c in weights:
        c.wait()

    def body(i, acc):
        ctr = cc[...]
        at_row = pl.multiple_of(48 * i, 16)
        tap = pl.multiple_of(960 * i, 16)
        masks = [x3[2, par, al, pl.ds(at_row + off, 256), :] == ctr for par, al, off in PLAN]
        out = []
        for g in range(2):
            lhs = jnp.concatenate([
                jnp.where(m, x3[g, par, al, pl.ds(at_row + off, 256), :], jnp.zeros((), BF))
                for m, (par, al, off) in zip(masks, PLAN)], axis=1)
            rhs = jnp.concatenate([
                jnp.concatenate([wb[g, pl.ds(tap + 240 * s + 80, 256), :], wb[g, pl.ds(tap + 240 * s, 256), :]], axis=1)
                for s in range(4)], axis=0)
            out.append(acc[g] + jnp.dot(lhs, rhs, preferred_element_type=F32))
        return tuple(out)
    acc = lax.fori_loop(0, 11, body, (jnp.zeros((256, 256), F32),) * 2)

    for g in range(2):
        halves = []
        for v in range(2):
            pos = acc[g][:, 128 * v:128 * v + 128] + bias_ref[g]
            own = src[g, 512:1024].reshape(32, 2, 8, 128)[:, v].reshape(256, 128)
            mark = src[2, 512:1024].reshape(32, 2, 8, 128)[:, v].reshape(256, 128)
            gel = 0.5 * pos * (1.0 + lax.erf(pos * R2))
            halves.append(jnp.where(mark >= 0.0, own + gel, 0.0).reshape(32, 1, 8, 128))
        res[g] = jnp.concatenate(halves, axis=1).reshape(512, 128)
        for c in range(NFS):
            fin[c, :, 128 * g:128 * g + 128] = res[g, pl.ds(c, 64, stride=8), :].astype(BF)
    ret[col] = fin[col]
    back = []
    for dq in range(1, NFS):
        to = at(0, dq)
        c = pltpu.make_async_remote_copy(src_ref=fin.at[to["fsdp"]], dst_ref=ret.at[col], send_sem=s2.at[dq],
                                         recv_sem=r2.at[dq], device_id=to, device_id_type=MESH)
        c.start()
        back.append(c)
    for c in back:
        c.wait()
    out_ref[0] = jnp.concatenate(
        [ret[q, :, 128 * g:128 * g + 80] for q in range(NFS) for g in range(2)], axis=1)


def pos_call(slabs, clip_lengths, pos_weight, bias):
    V = pl.BlockSpec(memory_space=pltpu.VMEM)
    A = pl.BlockSpec(memory_space=pl.ANY)
    D = pltpu.SemaphoreType.DMA
    lens = jnp.pad((clip_lengths[:, :, 0] // 320).astype(F32), ((0, 0), (0, 128 - NDP)))
    w = pos_weight.reshape(2, 128 * 80, 80)
    wb = jnp.pad(w, ((0, 0), (80, WROWS - 80 - 10240), (0, 48)))
    return pl.pallas_call(
        pos_kernel,
        out_shape=jax.ShapeDtypeStruct((1, 64, 1280), BF),
        in_specs=[V, V, V, A], out_specs=V,
        scratch_shapes=[pltpu.VMEM((3, 8, 64, 256), BF), pltpu.VMEM((3, 1552, 128), F32), pltpu.VMEM((3, 2, 2, 768, 256), BF),
                        pltpu.VMEM((256, 256), BF), pltpu.VMEM((2, WROWS, 128), BF), pltpu.VMEM((2, 512, 128), F32),
                        pltpu.VMEM((8, 64, 256), BF), pltpu.VMEM((8, 64, 256), BF),
                        D((2,)), D((23,)), D((23,)), D((8,)), D((8,))],
        compiler_params=pltpu.CompilerParams(vmem_limit_bytes=50 << 20, collective_id=1, has_side_effects=True),
        name="positional_conv",
    )(slabs, lens, bias, wb)


def per_device(waveform, clip_lengths, conv_first, conv_mid, conv_last, conv_gain, conv_shift, proj_gain, proj_shift,
               proj_weight, proj_bias, pos_weight, pos_bias):
    column = lax.axis_index("fsdp")
    slabs = encode_call(waveform, clip_lengths, conv_first, conv_mid, conv_last, conv_gain, conv_shift, proj_gain,
                        proj_shift, proj_weight, proj_bias)
    bias = lax.dynamic_slice_in_dim(pos_bias, column * 160, 160, 0)
    bias = jnp.pad(bias.reshape(2, 1, 80), ((0, 0), (0, 0), (0, 48)))
    return pos_call(slabs, clip_lengths, pos_weight, bias)


def solution(mesh):
    return jax.shard_map(
        per_device,
        mesh=mesh,
        in_specs=(P("fsdp", "dp", None),) + (P(),) * 10 + (P("fsdp", None, None, None), P()),
        out_specs=P("fsdp", "dp", None),
        check_vma=False,
    )
```

```python
import jax
import jax.numpy as jnp
from jax import lax
from jax.experimental import pallas as pl
from jax.experimental.pallas import tpu as pltpu
from jax.sharding import PartitionSpec as P

NORM_EPS = 1e-5
R2 = 0.7071067811865476
F32, BF = jnp.float32, jnp.bfloat16
MESH = pl.DeviceIdType.MESH
NDP, NFS = 32, 8


def norm_act(h, gain, shift):
    mean = jnp.sum(h, axis=-1, keepdims=True) * (1.0 / h.shape[-1])
    cen = h - mean
    var = jnp.sum(cen * cen, axis=-1, keepdims=True) * (1.0 / h.shape[-1])
    z = cen * lax.rsqrt(var + NORM_EPS) * gain + shift
    return (z * R2) * (1.0 + lax.erf(z))


WROWS = 133 * 80 + 16
PLAN = ((0, 0, 0), (1, 1, 0), (0, 1, 16), (1, 0, 32))


def encoder_kernel(wave_hbm, lens_hbm, w0_hbm, wm_hbm, wl_hbm, gain_hbm, shift_hbm, pg_hbm, ps_hbm, wp_hbm, pb_hbm, wk_hbm,
                   kb_hbm, out_ref, wave_v, lens_s, lens_v, w0_v, gain_v, shift_v, pg_v, ps_v, pb_v, kb_v, blk, blkb, send1,
                   recv1, send2, recv2, rows, xt, a0, a1, a2, a3, a4, a5, hal, fr, wm, wl, wp, slab, rcv, src, x3, cc, wraw, wt,
                   wb, res, fin, ret, wsem, msem, s1, r1, s2, r2, s3, r3, s4, r4):
    me, col = lax.axis_index("dp"), lax.axis_index("fsdp")
    peers = [(dr, dq) for dr in (0, 1, -1) for dq in range(NFS) if (dr, dq) != (0, 0)]

    def at(dr, dq):
        return {"dp": lax.rem(me + dr + NDP, NDP), "fsdp": lax.rem(col + dq + NFS, NFS)}
    barrier = pltpu.get_barrier_semaphore()
    greet = [{"dp": lax.rem(me + n, NDP)} for n in range(1, NDP)] + [at(dr, dq) for dr, dq in peers if dq]
    for to in greet:
        pl.semaphore_signal(barrier, inc=1, device_id=to, device_id_type=MESH)
    load_wave = pltpu.make_async_copy(wave_hbm, wave_v, msem.at[0])
    load_lens = pltpu.make_async_copy(lens_hbm, lens_s, msem.at[1])
    load_lens_v = pltpu.make_async_copy(lens_hbm, lens_v, msem.at[2])
    weights = [pltpu.make_async_copy(wk_hbm.at[g], wraw.at[g], wsem.at[7 + g]) for g in range(2)]
    pairs = ((w0_hbm, w0_v), (gain_hbm, gain_v), (shift_hbm, shift_v), (pg_hbm, pg_v), (ps_hbm, ps_v), (pb_hbm, pb_v), (kb_hbm, kb_v))
    small = [pltpu.make_async_copy(a, b, msem.at[3 + i]) for i, (a, b) in enumerate(pairs)]
    copies = [pltpu.make_async_copy(wm_hbm.at[i], wm.at[i], wsem.at[i]) for i in range(4)]
    copies += [pltpu.make_async_copy(wl_hbm.at[i], wl.at[i], wsem.at[4 + i]) for i in range(2)]
    copies += [pltpu.make_async_copy(wp_hbm, wp, wsem.at[6])]
    for c in [load_wave, load_lens, weights[0], load_lens_v, weights[1]] + small + copies:
        c.start()

    blk[...] = jnp.zeros((512, 128), F32)
    load_wave.wait()
    wave = wave_v[0].astype(F32)
    for r in range(10):
        blk[pl.ds(r, 30, stride=16), :] = wave[:, 128 * r:128 * r + 128]
    blk[pl.ds(10, 29, stride=16), :] = wave[1:30, 0:128]
    blkb[...] = blk[...].astype(BF).reshape(32, 16, 128)

    load_lens.wait()

    def tally(s, carry):
        total, mine, owners = carry[0], carry[1], carry[2:]
        mine = jnp.where(s == me, total, mine)
        total = total + lens_s[col, s]
        owners = tuple(o + jnp.where(total <= (me + NDP * j) * 1280, 1, 0) for j, o in enumerate(owners))
        return (total, mine) + owners
    zero = jnp.int32(0)
    counted = lax.fori_loop(0, NDP, tally, (zero,) * 18)
    start, owners = counted[1] // 1280, counted[2:]

    for t in range(NDP):
        send1[t] = blkb[(t - start) & 31]

    def turn(g):
        weights[g].wait()
        pad = jnp.zeros((48, 128), F32)

        def one(ii, c):
            for u in range(4):
                i = 4 * ii + u
                wt[pl.ds(i, 128, stride=80), :] = jnp.concatenate([wraw[g, i].astype(F32), pad], axis=0).T
            return c
        lax.fori_loop(0, 20, one, 0)

        def pack(r, c):
            wb[g, pl.ds(pl.multiple_of(80 + r * 512, 16), 512), :] = wt[pl.ds(pl.multiple_of(r * 512, 512), 512), :].astype(BF)
            return c
        lax.fori_loop(0, 20, pack, 0)
        wb[g, 0:80, :] = jnp.zeros((80, 128), BF)
        wb[g, 10320:WROWS, :] = jnp.zeros((WROWS - 10320, 128), BF)
    turn(0)
    recv1[me] = send1[me]
    pl.semaphore_wait(barrier, len(greet))
    first = []
    for n in range(1, NDP):
        to = lax.rem(me + n, NDP)
        c = pltpu.make_async_remote_copy(src_ref=send1.at[to], dst_ref=recv1.at[me], send_sem=s1.at[n],
                                         recv_sem=r1.at[n], device_id={"dp": to}, device_id_type=MESH)
        c.start()
        first.append(c)
    turn(1)
    for c in first:
        c.wait()
    half, slot = me // 16, me % 16
    for j in range(16):
        send2[j] = recv1[jnp.minimum(owners[j], 31)]
    second = []
    for j in range(16):
        to = 2 * j + half
        c = pltpu.make_async_remote_copy(src_ref=send2.at[j], dst_ref=recv2.at[slot], send_sem=s2.at[j],
                                         recv_sem=r2.at[slot], device_id={"dp": to}, device_id_type=MESH)
        second.append((to, c))

        @pl.when(to != me)
        def _():
            c.start()

        @pl.when(to == me)
        def _():
            recv2[slot] = send2[j]

    def spread(a):
        lane = lax.broadcasted_iota(jnp.int32, (768, 128), 1)
        full = src[a].reshape(97, 2, 8, 128)
        ev, od = full[:, 0].reshape(776, 128), full[:, 1].reshape(776, 128)
        for par in range(2):
            f0 = (ev if par == 0 else od)[0:768]
            f1 = od[0:768] if par == 0 else ev[8:776]
            f2 = (ev if par == 0 else od)[8:776]
            t1 = pltpu.roll(f1, 80, 1)
            t2 = pltpu.roll(f2, 32, 1)
            v0 = jnp.where(lane < 80, f0, t1)
            v1 = jnp.where(lane < 32, t1, jnp.where(lane < 112, t2, 0.0))
            v = jnp.concatenate([v0, v1], axis=1)
            x3[a, par, 0] = v.astype(BF)
            x3[a, par, 1, 0:752, :] = v[8:760].astype(BF)

    row = lax.broadcasted_iota(jnp.int32, (NDP, 128), 0)
    lane = lax.broadcasted_iota(jnp.int32, (NDP, 128), 1)
    upper = jnp.where(row <= lane, 1.0, 0.0).astype(BF)
    load_lens_v.wait()
    ends = jnp.dot((lens_v[...].astype(F32) * (1.0 / 320)).astype(BF), upper, preferred_element_type=F32)
    ends = jnp.where(lax.broadcasted_iota(jnp.int32, (8, 128), 1) < NDP, ends, 1e9)
    frame = lax.broadcasted_iota(jnp.int32, (195, 8, 128), 0) + (64 * me - 64)
    past = jnp.where(ends[None] <= frame.astype(F32), 1.0, 0.0)
    clip = jnp.sum(past, axis=2, keepdims=True)
    here, after = clip[0:194], clip[1:195]
    ok = (here == after) & (frame[0:194, :, 0:1] >= 0) & (here < NDP)
    src[2, 0:1552, :] = jnp.broadcast_to(jnp.where(ok, here, -1.0), (194, 8, 128)).reshape(1552, 128)
    spread(2)
    cc[...] = jnp.concatenate([src[2, 512:1024].reshape(32, 2, 8, 128)[:, 0].reshape(256, 128)] * 2, axis=1).astype(BF)
    odd = me % 2
    for i in range(16):
        c = pltpu.make_async_remote_copy(src_ref=send2.at[0], dst_ref=recv2.at[i], send_sem=s2.at[0],
                                         recv_sem=r2.at[i], device_id={"dp": me}, device_id_type=MESH)

        @pl.when(16 * odd + i != me)
        def _():
            c.wait_recv()
    for to, c in second:
        @pl.when(to != me)
        def _():
            c.wait_send()

    rows[...] = recv2[...].astype(F32).reshape(256, 128)
    flat = jnp.concatenate([rows[pl.ds(r, 16, stride=16), :] for r in range(11)], axis=1)
    y = jnp.concatenate([flat[:, 160 * e:160 * e + 256] for e in range(8)], axis=0)
    xt[...] = y.T
    halo = jnp.broadcast_to(rows[250:251, :], (16, 128))
    line = lax.broadcasted_iota(jnp.int32, (16, 128), 0)
    xh = halo
    for p in range(1, 15):
        xh = jnp.where(line == p, pltpu.roll(halo, 128 - 5 * p, 1), xh)

    dn = (((0,), (0,)), ((), ()))
    for c in small:
        c.wait()
    gains, shifts = gain_v[...] * R2, shift_v[...] * R2
    g0, b0 = gains[0:1], shifts[0:1]
    w0 = jnp.concatenate([w0_v[...].astype(F32), jnp.zeros((6, 512), F32)], axis=0).astype(BF)

    def put(li, v):
        for t in range(4):
            hal[li, t, 0:v.shape[0], :] = v[:, 128 * t:128 * t + 128]

    def pick(li, begin, size, stride=1):
        ds = pl.ds(begin, size, stride=stride) if stride > 1 else pl.ds(begin, size)
        return jnp.concatenate([hal[li, t, ds, :] for t in range(4)], axis=1)

    h = jnp.dot(xh[:, 0:16].astype(BF), w0, preferred_element_type=F32)
    hal[...] = jnp.zeros(hal.shape, F32)
    put(0, norm_act(h, g0, b0))

    def l0(i, c):
        win = jnp.concatenate([xt[pl.ds(20 * i + 5 * q, 16), :] for q in range(4)], axis=1).astype(BF)
        h = lax.dot_general(win, w0, dn, preferred_element_type=F32)
        a = norm_act(h, g0, b0).astype(BF).reshape(4, 4, 2, 16, 512)
        for q in range(4):
            a0[4 * i + q] = a[q, :, 0].reshape(64, 512)
            a0[4 * i + q + 32] = a[q, :, 1].reshape(64, 512)
        return c
    lax.fori_loop(0, 8, l0, 0)

    srcs = [a0, a1, a2, a3, a4, a5]
    counts = [32, 16, 8, 4, 2, 1]
    for L in range(1, 7):
        inp, n = srcs[L - 1], counts[L - 1]
        K = 3 if L <= 4 else 2
        G = min(8, n)
        copies[L - 1].wait()
        w = (lambda L=L: wm[L - 1].reshape(1536, 512)) if L <= 4 else (lambda L=L: wl[L - 5].reshape(1024, 512))
        g, s = gains[L:L + 1], shifts[L:L + 1]
        if K == 3:
            v = inp[0].astype(F32)
            inp[2 * n] = jnp.concatenate([v[16:64], v[1:16], pick(L - 1, 0, 1)], axis=0).astype(BF)

        def body(i, c, inp=inp, K=K, G=G, w=w, g=g, s=s, L=L, halo=False):
            taps = []
            for k in range(K):
                lhs = [inp[2 * (G * i + q) + k] for q in range(G)]
                if halo:
                    lhs.append(jnp.concatenate([pick(L - 1, k, 8, 2), jnp.zeros((8, 512), F32)], axis=0).astype(BF))
                taps.append(jnp.concatenate(lhs, axis=0) if len(lhs) > 1 else lhs[0])
            a = norm_act(jnp.dot(jnp.concatenate(taps, axis=1), w(), preferred_element_type=F32), g, s)
            if halo:
                put(L, a[64 * G:64 * G + 8])
            if L == 6:
                return a
            for q in range(G):
                srcs[L][G * i + q] = a[64 * q:64 * q + 64].astype(BF)
            return c
        last = body(0, 0, halo=(L <= 3))
        if n // G > 1:
            lax.fori_loop(1, n // G, body, 0)

    v = last.astype(BF).astype(F32)
    for t in range(4):
        for q in range(4):
            fr[t, pl.ds(q, 16, stride=4), :] = v[16 * q:16 * q + 16, 128 * t:128 * t + 128]
    v = jnp.concatenate([fr[t] for t in range(4)], axis=1)
    mean = jnp.sum(v, axis=-1, keepdims=True) * (1.0 / 512)
    cen = v - mean
    var = jnp.sum(cen * cen, axis=-1, keepdims=True) * (1.0 / 512)
    nf = (cen * lax.rsqrt(var + NORM_EPS) * pg_v[...] + ps_v[...]).astype(BF)
    copies[6].wait()
    pr = jnp.dot(nf, wp[...], preferred_element_type=F32) + jnp.concatenate([pb_v[r:r + 1, :] for r in range(10)], axis=1)
    gap = jnp.zeros((64, 48), F32)
    for q in range(8):
        parts = []
        for g in range(2):
            parts += [pr[:, 160 * q + 80 * g:160 * q + 80 * g + 80], gap]
        slab[q] = jnp.concatenate(parts, axis=1).astype(BF)
    rcv[1, col] = slab[col]
    sends = []
    for n, (dr, dq) in enumerate(peers):
        to = at(dr, dq)
        c = pltpu.make_async_remote_copy(src_ref=slab.at[to["fsdp"]], dst_ref=rcv.at[1 - dr, col],
                                         send_sem=s3.at[n], recv_sem=r3.at[n], device_id=to, device_id_type=MESH)
        c.start()
        sends.append(c)

    flat = jnp.concatenate([kb_v[r:r + 1, :] for r in range(10)] + [jnp.zeros((1, 128), F32)], axis=1)
    bias = []
    for g in range(2):
        b = jnp.zeros((1, 128), F32)
        for q in range(NFS):
            b = jnp.where(col == q, flat[:, 160 * q + 80 * g:160 * q + 80 * g + 128], b)
        bias.append(b)
    for c in sends:
        c.wait()

    for g in range(2):
        src[g, 1536:1552, :] = jnp.zeros((16, 128), F32)
        for part in range(3):
            for c in range(NFS):
                src[g, pl.ds(512 * part + c, 64, stride=8), :] = rcv[part, c, :, 128 * g:128 * g + 128].astype(F32)
    spread(0)
    spread(1)

    def body(i, acc):
        ctr = cc[...]
        at_row = pl.multiple_of(48 * i, 16)
        tap = pl.multiple_of(960 * i, 16)
        masks = [x3[2, par, al, pl.ds(at_row + off, 256), :] == ctr for par, al, off in PLAN]
        out = []
        for g in range(2):
            lhs = jnp.concatenate([
                jnp.where(m, x3[g, par, al, pl.ds(at_row + off, 256), :], jnp.zeros((), BF))
                for m, (par, al, off) in zip(masks, PLAN)], axis=1)
            rhs = jnp.concatenate([
                jnp.concatenate([wb[g, pl.ds(tap + 240 * s + 80, 256), :], wb[g, pl.ds(tap + 240 * s, 256), :]], axis=1)
                for s in range(4)], axis=0)
            out.append(acc[g] + jnp.dot(lhs, rhs, preferred_element_type=F32))
        return tuple(out)
    acc = lax.fori_loop(0, 11, body, (jnp.zeros((256, 256), F32),) * 2)

    for g in range(2):
        halves = []
        for v in range(2):
            pos = acc[g][:, 128 * v:128 * v + 128] + bias[g]
            own = src[g, 512:1024].reshape(32, 2, 8, 128)[:, v].reshape(256, 128)
            mark = src[2, 512:1024].reshape(32, 2, 8, 128)[:, v].reshape(256, 128)
            gel = 0.5 * pos * (1.0 + lax.erf(pos * R2))
            halves.append(jnp.where(mark >= 0.0, own + gel, 0.0).reshape(32, 1, 8, 128))
        res[g] = jnp.concatenate(halves, axis=1).reshape(512, 128)
        for c in range(NFS):
            fin[c, :, 128 * g:128 * g + 128] = res[g, pl.ds(c, 64, stride=8), :].astype(BF)
    ret[col] = fin[col]
    back = []
    for dq in range(1, NFS):
        to = at(0, dq)
        c = pltpu.make_async_remote_copy(src_ref=fin.at[to["fsdp"]], dst_ref=ret.at[col], send_sem=s4.at[dq],
                                         recv_sem=r4.at[dq], device_id=to, device_id_type=MESH)
        c.start()
        back.append(c)
    for c in back:
        c.wait()
    out_ref[0] = jnp.concatenate(
        [ret[q, :, 128 * g:128 * g + 80] for q in range(NFS) for g in range(2)], axis=1)


def per_device(waveform, clip_lengths, conv_first, conv_mid, conv_last, conv_gain, conv_shift, proj_gain, proj_shift,
               proj_weight, proj_bias, pos_weight, pos_bias):
    H = pl.BlockSpec(memory_space=pltpu.HBM)
    D = pltpu.SemaphoreType.DMA
    V = pltpu.VMEM
    return pl.pallas_call(
        encoder_kernel,
        out_shape=jax.ShapeDtypeStruct((1, 64, 1280), BF),
        in_specs=[H] * 13,
        out_specs=pl.BlockSpec(memory_space=pltpu.VMEM),
        scratch_shapes=[V((1, 30, 1280), BF), pltpu.SMEM((8, 32), jnp.int32), V((8, 32), jnp.int32), V((10, 512), BF), V((7, 512), F32),
                        V((7, 512), F32), V((1, 512), F32), V((1, 512), F32), V((10, 128), F32), V((10, 128), F32),
                        V((512, 128), F32), V((32, 16, 128), BF), V((32, 16, 128), BF),
                        V((32, 16, 128), BF), V((16, 16, 128), BF), V((16, 16, 128), BF),
                        V((256, 128), F32), V((256, 128), F32),
                        V((65, 64, 512), BF), V((33, 64, 512), BF), V((17, 64, 512), BF),
                        V((9, 64, 512), BF), V((4, 64, 512), BF), V((2, 64, 512), BF),
                        V((4, 4, 24, 128), F32), V((4, 64, 128), F32),
                        V((4, 3, 512, 512), BF), V((2, 2, 512, 512), BF), V((512, 1280), BF),
                        V((8, 64, 256), BF), V((3, 8, 64, 256), BF), V((3, 1552, 128), F32), V((3, 2, 2, 768, 256), BF),
                        V((256, 256), BF), V((2, 80, 80, 128), BF), V((10240, 128), F32), V((2, WROWS, 128), BF), V((2, 512, 128), F32),
                        V((8, 64, 256), BF), V((8, 64, 256), BF),
                        D((9,)), D((10,)), D((32,)), D((32,)), D((16,)), D((16,)), D((23,)), D((23,)), D((8,)), D((8,))],
        compiler_params=pltpu.CompilerParams(vmem_limit_bytes=62 << 20, collective_id=0, has_side_effects=True),
        name="encoder",
    )(waveform, clip_lengths[:, :, 0], conv_first, conv_mid, conv_last, conv_gain, conv_shift, proj_gain[None], proj_shift[None],
      proj_weight, proj_bias.reshape(10, 128), jnp.transpose(pos_weight, (0, 2, 3, 1)), pos_bias.reshape(10, 128))


def solution(mesh):
    return jax.shard_map(
        per_device,
        mesh=mesh,
        in_specs=(P("fsdp", "dp", None),) + (P(),) * 10 + (P("fsdp", None, None, None), P()),
        out_specs=P("fsdp", "dp", None),
        check_vma=False,
    )
```

```python
import jax
import jax.numpy as jnp
from jax import lax
from jax.experimental import pallas as pl
from jax.experimental.pallas import tpu as pltpu
from jax.sharding import PartitionSpec as P

NORM_EPS = 1e-5
R2 = 0.7071067811865476
F32, BF = jnp.float32, jnp.bfloat16
MESH = pl.DeviceIdType.MESH
NDP, NFS = 32, 8


def norm_act(h, gain, shift):
    mean = jnp.sum(h, axis=-1, keepdims=True) * (1.0 / h.shape[-1])
    cen = h - mean
    var = jnp.sum(cen * cen, axis=-1, keepdims=True) * (1.0 / h.shape[-1])
    z = cen * lax.rsqrt(var + NORM_EPS) * gain + shift
    return (z * R2) * (1.0 + lax.erf(z))


VMEM_MB = 58
WROWS = 133 * 80 + 16
PLAN = ((0, 0, 0), (1, 1, 0), (0, 1, 16), (1, 0, 32))


def encoder_kernel(wave_hbm, lens_hbm, w0_hbm, wm_hbm, wl_hbm, gain_hbm, shift_hbm, pg_hbm, ps_hbm, wp_hbm, pb_hbm, wk_hbm,
                   kb_hbm, out_ref, wave_v, lens_s, lens_v, w0_v, gain_v, shift_v, pg_v, ps_v, pb_v, kb_v, blk, blkb, send1,
                   recv1, send2, recv2, rows, xt, a0, a1, a2, a3, a4, a5, hal, fr, wm, wl, wp, slab, rcv, src, x3, cc, wraw, wt,
                   wb, res, fin, ret, part, wsem, msem, s1, r1, s2, r2, s3, r3, s4, r4):
    me, col = lax.axis_index("dp"), lax.axis_index("fsdp")
    peers = [(dr, dq) for dr in (0, 1, -1) for dq in (4, 5, 3, 6, 2, 7, 1, 0) if (dr, dq) != (0, 0)]
    steps = sorted([(dz, dy) for dz in range(8) for dy in range(4) if dz or dy],
                   key=lambda s: -(min(s[0], 8 - s[0]) + min(s[1], 4 - s[1])))

    def at(dr, dq):
        return {"dp": (me + dr) & (NDP - 1), "fsdp": (col + dq) & (NFS - 1)}

    def hop(dz, dy):
        return (((me >> 2) + dz) & 7) * 4 + ((me + dy) & 3)

    def residue(d):
        return 16 * (1 - (d & 1)) + 2 * (d >> 2) + ((d & 3) >> 1)
    barrier = pltpu.get_barrier_semaphore()
    greet = [{"dp": hop(dz, dy)} for dz, dy in steps] + [at(dr, dq) for dr, dq in peers if dq]
    for to in greet:
        pl.semaphore_signal(barrier, inc=1, device_id=to, device_id_type=MESH)
    load_wave = pltpu.make_async_copy(wave_hbm, wave_v, msem.at[0])
    load_lens = pltpu.make_async_copy(lens_hbm, lens_s, msem.at[1])
    load_lens_v = pltpu.make_async_copy(lens_hbm, lens_v, msem.at[2])
    weights = [pltpu.make_async_copy(wk_hbm.at[g], wraw.at[g], wsem.at[7 + g]) for g in range(2)]
    pairs = ((w0_hbm, w0_v), (gain_hbm, gain_v), (shift_hbm, shift_v), (pg_hbm, pg_v), (ps_hbm, ps_v), (pb_hbm, pb_v), (kb_hbm, kb_v))
    small = [pltpu.make_async_copy(a, b, msem.at[3 + i]) for i, (a, b) in enumerate(pairs)]
    copies = [pltpu.make_async_copy(wm_hbm.at[i], wm.at[i], wsem.at[i]) for i in range(4)]
    copies += [pltpu.make_async_copy(wl_hbm.at[i], wl.at[i], wsem.at[4 + i]) for i in range(2)]
    copies += [pltpu.make_async_copy(wp_hbm, wp, wsem.at[6])]
    for c in [load_wave, load_lens, weights[0], load_lens_v, weights[1]] + small + copies:
        c.start()

    blk[...] = jnp.zeros((512, 128), F32)
    load_wave.wait()
    wave = wave_v[0].astype(F32)
    for r in range(10):
        blk[pl.ds(r, 30, stride=16), :] = wave[:, 128 * r:128 * r + 128]
    blk[pl.ds(10, 29, stride=16), :] = wave[1:30, 0:128]
    blkb[...] = blk[...].astype(BF).reshape(32, 16, 128)

    load_lens.wait()

    mine_mod = residue(me)

    def tally(s, carry):
        total, mine, owners = carry[0], carry[1], carry[2:]
        mine = jnp.where(s == me, total, mine)
        total = total + lens_s[col, s]
        owners = tuple(o + jnp.where(total <= (mine_mod + NDP * j) * 1280, 1, 0) for j, o in enumerate(owners))
        return (total, mine) + owners
    zero = jnp.int32(0)
    counted = lax.fori_loop(0, NDP, tally, (zero,) * 18)
    start, owners = counted[1] // 1280, counted[2:]

    for t in range(NDP):
        send1[t] = blkb[(residue(t) - start) & 31]

    def turn(g):
        weights[g].wait()
        pad = jnp.zeros((48, 128), F32)

        def one(ii, c):
            for u in range(4):
                i = 4 * ii + u
                wt[pl.ds(i, 128, stride=80), :] = jnp.concatenate([wraw[g, i].astype(F32), pad], axis=0).T
            return c
        lax.fori_loop(0, 20, one, 0)

        def pack(r, c):
            wb[g, pl.ds(pl.multiple_of(80 + r * 512, 16), 512), :] = wt[pl.ds(pl.multiple_of(r * 512, 512), 512), :].astype(BF)
            return c
        lax.fori_loop(0, 20, pack, 0)
        wb[g, 0:80, :] = jnp.zeros((80, 128), BF)
        wb[g, 10320:WROWS, :] = jnp.zeros((WROWS - 10320, 128), BF)
    turn(0)
    recv1[me] = send1[me]
    pl.semaphore_wait(barrier, len(greet))
    first = []
    for n, (dz, dy) in enumerate(steps):
        to = hop(dz, dy)
        c = pltpu.make_async_remote_copy(src_ref=send1.at[to], dst_ref=recv1.at[me], send_sem=s1.at[n],
                                         recv_sem=r1.at[n], device_id={"dp": to}, device_id_type=MESH)
        c.start()
        first.append(c)
    turn(1)
    for c in first:
        c.wait()
    half, slot = mine_mod >> 4, mine_mod & 15
    for j in range(16):
        send2[j] = recv1[jnp.minimum(owners[j], 31)]
    second = []
    for n in (4, 3, 5, 2, 6, 1, 7, 0):
        for m in range(2):
            j = (((me >> 2) + n) & 7) * 2 + m
            to = 2 * j + half
            c = pltpu.make_async_remote_copy(src_ref=send2.at[j], dst_ref=recv2.at[slot], send_sem=s2.at[j],
                                             recv_sem=r2.at[slot], device_id={"dp": to}, device_id_type=MESH)
            c.start()
            second.append(c)

    def spread(a, lo, hi):
        n = hi - lo + (1 if hi < 96 else 0)
        lane = lax.broadcasted_iota(jnp.int32, (8 * n, 128), 1)
        full = src[a, 16 * lo:16 * (lo + n + 1), :].reshape(n + 1, 2, 8, 128)
        ev, od = full[:, 0].reshape(8 * n + 8, 128), full[:, 1].reshape(8 * n + 8, 128)
        for par in range(2):
            f0 = (ev if par == 0 else od)[0:8 * n]
            f1 = od[0:8 * n] if par == 0 else ev[8:8 * n + 8]
            f2 = (ev if par == 0 else od)[8:8 * n + 8]
            t1 = pltpu.roll(f1, 80, 1)
            t2 = pltpu.roll(f2, 32, 1)
            v0 = jnp.where(lane < 80, f0, t1)
            v1 = jnp.where(lane < 32, t1, jnp.where(lane < 112, t2, 0.0))
            v = jnp.concatenate([v0, v1], axis=1)
            m = 8 * (hi - lo)
            x3[a, par, 0, 8 * lo:8 * lo + m, :] = v[0:m].astype(BF)
            k = m if hi < 96 else m - 16
            x3[a, par, 1, 8 * lo:8 * lo + k, :] = v[8:8 + k].astype(BF)

    row = lax.broadcasted_iota(jnp.int32, (NDP, 128), 0)
    lane = lax.broadcasted_iota(jnp.int32, (NDP, 128), 1)
    upper = jnp.where(row <= lane, 1.0, 0.0).astype(BF)
    load_lens_v.wait()
    ends = jnp.dot((lens_v[...].astype(F32) * (1.0 / 320)).astype(BF), upper, preferred_element_type=F32)
    ends = jnp.where(lax.broadcasted_iota(jnp.int32, (8, 128), 1) < NDP, ends, 1e9)
    frame = lax.broadcasted_iota(jnp.int32, (195, 8, 128), 0) + (64 * me - 64)
    past = jnp.where(ends[None] <= frame.astype(F32), 1.0, 0.0)
    clip = jnp.sum(past, axis=2, keepdims=True)
    here, after = clip[0:194], clip[1:195]
    ok = (here == after) & (frame[0:194, :, 0:1] >= 0) & (here < NDP)
    src[2, 0:1552, :] = jnp.broadcast_to(jnp.where(ok, here, -1.0), (194, 8, 128)).reshape(1552, 128)
    spread(2, 0, 96)
    cc[...] = jnp.concatenate([src[2, 512:1024].reshape(32, 2, 8, 128)[:, 0].reshape(256, 128)] * 2, axis=1).astype(BF)
    for i in range(16):
        pltpu.make_async_remote_copy(src_ref=send2.at[0], dst_ref=recv2.at[i], send_sem=s2.at[0],
                                     recv_sem=r2.at[i], device_id={"dp": me}, device_id_type=MESH).wait_recv()
    for c in second:
        c.wait_send()

    rows[...] = recv2[...].astype(F32).reshape(256, 128)
    flat = jnp.concatenate([rows[pl.ds(r, 16, stride=16), :] for r in range(11)], axis=1)
    y = jnp.concatenate([flat[:, 160 * e:160 * e + 256] for e in range(8)], axis=0)
    xt[...] = y.T
    halo = jnp.broadcast_to(rows[250:251, :], (16, 128))
    line = lax.broadcasted_iota(jnp.int32, (16, 128), 0)
    xh = halo
    for p in range(1, 15):
        xh = jnp.where(line == p, pltpu.roll(halo, 128 - 5 * p, 1), xh)

    dn = (((0,), (0,)), ((), ()))
    for c in small:
        c.wait()
    gains, shifts = gain_v[...] * R2, shift_v[...] * R2
    g0, b0 = gains[0:1], shifts[0:1]
    w0 = jnp.concatenate([w0_v[...].astype(F32), jnp.zeros((6, 512), F32)], axis=0).astype(BF)

    def put(li, v):
        for t in range(4):
            hal[li, t, 0:v.shape[0], :] = v[:, 128 * t:128 * t + 128]

    def pick(li, begin, size, stride=1):
        ds = pl.ds(begin, size, stride=stride) if stride > 1 else pl.ds(begin, size)
        return jnp.concatenate([hal[li, t, ds, :] for t in range(4)], axis=1)

    h = jnp.dot(xh[:, 0:16].astype(BF), w0, preferred_element_type=F32)
    hal[...] = jnp.zeros(hal.shape, F32)
    put(0, norm_act(h, g0, b0))

    def l0(i, c):
        win = jnp.concatenate([xt[pl.ds(20 * i + 5 * q, 16), :] for q in range(4)], axis=1).astype(BF)
        h = lax.dot_general(win, w0, dn, preferred_element_type=F32)
        a = norm_act(h, g0, b0).astype(BF).reshape(4, 4, 2, 16, 512)
        for q in range(4):
            a0[4 * i + q] = a[q, :, 0].reshape(64, 512)
            a0[4 * i + q + 32] = a[q, :, 1].reshape(64, 512)
        return c
    lax.fori_loop(0, 8, l0, 0)

    srcs = [a0, a1, a2, a3, a4, a5]
    counts = [32, 16, 8, 4, 2, 1]
    for L in range(1, 7):
        inp, n = srcs[L - 1], counts[L - 1]
        K = 3 if L <= 4 else 2
        G = min(8, n)
        copies[L - 1].wait()
        w = (lambda L=L: wm[L - 1].reshape(1536, 512)) if L <= 4 else (lambda L=L: wl[L - 5].reshape(1024, 512))
        g, s = gains[L:L + 1], shifts[L:L + 1]
        if K == 3:
            v = inp[0].astype(F32)
            inp[2 * n] = jnp.concatenate([v[16:64], v[1:16], pick(L - 1, 0, 1)], axis=0).astype(BF)

        def body(i, c, inp=inp, K=K, G=G, w=w, g=g, s=s, L=L, halo=False):
            taps = []
            for k in range(K):
                lhs = [inp[2 * (G * i + q) + k] for q in range(G)]
                if halo:
                    lhs.append(jnp.concatenate([pick(L - 1, k, 8, 2), jnp.zeros((8, 512), F32)], axis=0).astype(BF))
                taps.append(jnp.concatenate(lhs, axis=0) if len(lhs) > 1 else lhs[0])
            a = norm_act(jnp.dot(jnp.concatenate(taps, axis=1), w(), preferred_element_type=F32), g, s)
            if halo:
                put(L, a[64 * G:64 * G + 8])
            if L == 6:
                return a
            for q in range(G):
                srcs[L][G * i + q] = a[64 * q:64 * q + 64].astype(BF)
            return c
        last = body(0, 0, halo=(L <= 3))
        if n // G > 1:
            lax.fori_loop(1, n // G, body, 0)

    v = last.astype(BF).astype(F32)
    for t in range(4):
        for q in range(4):
            fr[t, pl.ds(q, 16, stride=4), :] = v[16 * q:16 * q + 16, 128 * t:128 * t + 128]
    v = jnp.concatenate([fr[t] for t in range(4)], axis=1)
    mean = jnp.sum(v, axis=-1, keepdims=True) * (1.0 / 512)
    cen = v - mean
    var = jnp.sum(cen * cen, axis=-1, keepdims=True) * (1.0 / 512)
    nf = (cen * lax.rsqrt(var + NORM_EPS) * pg_v[...] + ps_v[...]).astype(BF)
    copies[6].wait()
    pr = jnp.dot(nf, wp[...], preferred_element_type=F32) + jnp.concatenate([pb_v[r:r + 1, :] for r in range(10)], axis=1)
    for q in range(8):
        v = pr[:, 160 * q:160 * q + 160]
        rest = jnp.concatenate([v[16 * b:16 * b + 16, 128:160] for b in range(4)], axis=1)
        slab[q] = jnp.concatenate([v[:, 0:128], rest], axis=0).astype(BF)
    rcv[1, col] = slab[col]
    sends = []
    for n, (dr, dq) in enumerate(peers):
        to = at(dr, dq)
        c = pltpu.make_async_remote_copy(src_ref=slab.at[to["fsdp"]], dst_ref=rcv.at[1 - dr, col],
                                         send_sem=s3.at[n], recv_sem=r3.at[n], device_id=to, device_id_type=MESH)
        c.start()
        sends.append(c)

    flat = jnp.concatenate([kb_v[r:r + 1, :] for r in range(10)] + [jnp.zeros((1, 128), F32)], axis=1)
    bias = []
    for g in range(2):
        b = jnp.zeros((1, 128), F32)
        for q in range(NFS):
            b = jnp.where(col == q, flat[:, 160 * q + 80 * g:160 * q + 80 * g + 128], b)
        bias.append(b)
    low = lax.broadcasted_iota(jnp.int32, (64, 128), 1) < 48

    def interleave(part):
        for c in range(NFS):
            v = rcv[part, c].astype(F32)
            rest = jnp.concatenate([pltpu.roll(v[64:80], (176 - 32 * b) & 127, 1) for b in range(4)], axis=0)
            src[0, pl.ds(512 * part + c, 64, stride=8), :] = v[0:64]
            src[1, pl.ds(512 * part + c, 64, stride=8), :] = jnp.where(low, pltpu.roll(v[0:64], 48, 1), rest)
    for g in range(2):
        src[g, 1536:1552, :] = jnp.zeros((16, 128), F32)
    for c in sends[0:15]:
        c.wait_recv()
    interleave(0)
    interleave(1)
    for g in range(2):
        spread(g, 0, 60)

    def taps(groups):
        def body(i, acc):
            ctr = cc[...]
            at_row = pl.multiple_of(48 * i, 16)
            tap = pl.multiple_of(960 * i, 16)
            masks = [x3[2, par, al, pl.ds(at_row + off, 256), :] == ctr for par, al, off in PLAN]
            out = []
            for n, g in enumerate(groups):
                lhs = jnp.concatenate([
                    jnp.where(m, x3[g, par, al, pl.ds(at_row + off, 256), :], jnp.zeros((), BF))
                    for m, (par, al, off) in zip(masks, PLAN)], axis=1)
                rhs = jnp.concatenate([
                    jnp.concatenate([wb[g, pl.ds(tap + 240 * s + 80, 256), :], wb[g, pl.ds(tap + 240 * s, 256), :]], axis=1)
                    for s in range(4)], axis=0)
                out.append(acc[n] + jnp.dot(lhs, rhs, preferred_element_type=F32))
            return tuple(out)
        return body
    acc = lax.fori_loop(0, 5, taps((0, 1)), (jnp.zeros((256, 256), F32),) * 2)
    part[...] = acc[1]
    for c in sends[15:23]:
        c.wait_recv()
    interleave(2)
    for g in range(2):
        spread(g, 60, 96)

    back = []
    for g in range(2):
        a = lax.fori_loop(5, 11, taps((g,)), ((acc[0] if g == 0 else part[...]),))[0]
        halves = []
        for v in range(2):
            pos = a[:, 128 * v:128 * v + 128] + bias[g]
            own = src[g, 512:1024].reshape(32, 2, 8, 128)[:, v].reshape(256, 128)
            mark = src[2, 512:1024].reshape(32, 2, 8, 128)[:, v].reshape(256, 128)
            gel = 0.5 * pos * (1.0 + lax.erf(pos * R2))
            halves.append(jnp.where(mark >= 0.0, own + gel, 0.0).reshape(32, 1, 8, 128))
        res[g] = jnp.concatenate(halves, axis=1).reshape(512, 128)
        for c in range(NFS):
            fin[g, c] = res[g, pl.ds(c, 64, stride=8), :].astype(BF)
        ret[g, col] = fin[g, col]
        for n, dq in enumerate((4, 5, 3, 6, 2, 7, 1)):
            to = at(0, dq)
            c = pltpu.make_async_remote_copy(src_ref=fin.at[g, to["fsdp"]], dst_ref=ret.at[g, col], send_sem=s4.at[g, n],
                                             recv_sem=r4.at[g, n], device_id=to, device_id_type=MESH)
            c.start()
            back.append(c)
    for c in sends:
        c.wait_send()
    for c in back:
        c.wait()
    out_ref[0] = jnp.concatenate([ret[g, q, :, 0:80] for q in range(NFS) for g in range(2)], axis=1)


def per_device(waveform, clip_lengths, conv_first, conv_mid, conv_last, conv_gain, conv_shift, proj_gain, proj_shift,
               proj_weight, proj_bias, pos_weight, pos_bias):
    H = pl.BlockSpec(memory_space=pltpu.HBM)
    D = pltpu.SemaphoreType.DMA
    V = pltpu.VMEM
    return pl.pallas_call(
        encoder_kernel,
        out_shape=jax.ShapeDtypeStruct((1, 64, 1280), BF),
        in_specs=[H] * 13,
        out_specs=pl.BlockSpec(memory_space=pltpu.VMEM),
        scratch_shapes=[V((1, 30, 1280), BF), pltpu.SMEM((8, 32), jnp.int32), V((8, 32), jnp.int32), V((10, 512), BF), V((7, 512), F32),
                        V((7, 512), F32), V((1, 512), F32), V((1, 512), F32), V((10, 128), F32), V((10, 128), F32),
                        V((512, 128), F32), V((32, 16, 128), BF), V((32, 16, 128), BF),
                        V((32, 16, 128), BF), V((16, 16, 128), BF), V((16, 16, 128), BF),
                        V((256, 128), F32), V((256, 128), F32),
                        V((65, 64, 512), BF), V((33, 64, 512), BF), V((17, 64, 512), BF),
                        V((9, 64, 512), BF), V((4, 64, 512), BF), V((2, 64, 512), BF),
                        V((4, 4, 24, 128), F32), V((4, 64, 128), F32),
                        V((4, 3, 512, 512), BF), V((2, 2, 512, 512), BF), V((512, 1280), BF),
                        V((8, 80, 128), BF), V((3, 8, 80, 128), BF), V((3, 1552, 128), F32), V((3, 2, 2, 768, 256), BF),
                        V((256, 256), BF), V((2, 80, 80, 128), BF), V((10240, 128), F32), V((2, WROWS, 128), BF), V((2, 512, 128), F32),
                        V((2, 8, 64, 128), BF), V((2, 8, 64, 128), BF), V((256, 256), F32),
                        D((9,)), D((10,)), D((32,)), D((32,)), D((16,)), D((16,)), D((23,)), D((23,)), D((2, 7)), D((2, 7))],
        compiler_params=pltpu.CompilerParams(vmem_limit_bytes=VMEM_MB << 20, collective_id=0, has_side_effects=True),
        name="encoder",
    )(waveform, clip_lengths[:, :, 0], conv_first, conv_mid, conv_last, conv_gain, conv_shift, proj_gain[None], proj_shift[None],
      proj_weight, proj_bias.reshape(10, 128), jnp.transpose(pos_weight, (0, 2, 3, 1)), pos_bias.reshape(10, 128))


def solution(mesh):
    return jax.shard_map(
        per_device,
        mesh=mesh,
        in_specs=(P("fsdp", "dp", None),) + (P(),) * 10 + (P("fsdp", None, None, None), P()),
        out_specs=P("fsdp", "dp", None),
        check_vma=False,
    )
```

```python
import jax
import jax.numpy as jnp
from jax import lax
from jax.experimental import pallas as pl
from jax.experimental.pallas import tpu as pltpu
from jax.sharding import PartitionSpec as P

NORM_EPS = 1e-5
R2 = 0.7071067811865476
F32, BF = jnp.float32, jnp.bfloat16
MESH = pl.DeviceIdType.MESH
NDP, NFS = 32, 8


def norm_act(h, gain, shift, eps):
    var = jnp.sum(h * h, axis=-1, keepdims=True) * (1.0 / h.shape[-1])
    z = h * lax.rsqrt(var + eps) * gain + shift
    return z + z * lax.erf(z)


VMEM_MB = 58
WROWS = 133 * 80 + 16
PLAN = ((0, 0, 0), (1, 1, 0), (0, 1, 16), (1, 0, 32))


def encoder_kernel(wave_hbm, lens_hbm, w0_hbm, wm_hbm, wl_hbm, gain_hbm, shift_hbm, pg_hbm, ps_hbm, wp_hbm, pb_hbm, wk_hbm,
                   kb_hbm, out_ref, wave_v, lens_s, lens_v, w0_v, gain_v, shift_v, pg_v, ps_v, pb_v, kb_v, blk, blkb, send1,
                   recv1, send2, recv2, rows, xt, a0, a1, a2, a3, a4, a5, hal, fr, wm, wl, wp, slab, rcv, src, x3, cc, wraw, wt,
                   wb, res, fin, ret, part, wsem, msem, s1, r1, s2, r2, s3, r3, s4, r4):
    me, col = lax.axis_index("dp"), lax.axis_index("fsdp")
    peers = [(dr, dq) for dr in (0, 1, -1) for dq in (4, 5, 3, 6, 2, 7, 1, 0) if (dr, dq) != (0, 0)]
    steps = sorted([(dz, dy) for dz in range(8) for dy in range(4) if dz or dy],
                   key=lambda s: -(min(s[0], 8 - s[0]) + min(s[1], 4 - s[1])))

    def at(dr, dq):
        return {"dp": (me + dr) & (NDP - 1), "fsdp": (col + dq) & (NFS - 1)}

    def hop(dz, dy):
        return (((me >> 2) + dz) & 7) * 4 + ((me + dy) & 3)

    def residue(d):
        return 16 * (1 - (d & 1)) + 2 * (d >> 2) + ((d & 3) >> 1)
    barrier = pltpu.get_barrier_semaphore()
    greet = [{"dp": hop(dz, dy)} for dz, dy in steps] + [at(dr, dq) for dr, dq in peers if dq]
    for to in greet:
        pl.semaphore_signal(barrier, inc=1, device_id=to, device_id_type=MESH)
    load_wave = pltpu.make_async_copy(wave_hbm, wave_v, msem.at[0])
    load_lens = pltpu.make_async_copy(lens_hbm, lens_s, msem.at[1])
    load_lens_v = pltpu.make_async_copy(lens_hbm, lens_v, msem.at[2])
    weights = [pltpu.make_async_copy(wk_hbm.at[g], wraw.at[g], wsem.at[7 + g]) for g in range(2)]
    pairs = ((w0_hbm, w0_v), (gain_hbm, gain_v), (shift_hbm, shift_v), (pg_hbm, pg_v), (ps_hbm, ps_v), (pb_hbm, pb_v), (kb_hbm, kb_v))
    small = [pltpu.make_async_copy(a, b, msem.at[3 + i]) for i, (a, b) in enumerate(pairs)]
    copies = [pltpu.make_async_copy(wm_hbm.at[i], wm.at[i], wsem.at[i]) for i in range(4)]
    copies += [pltpu.make_async_copy(wl_hbm.at[i], wl.at[i], wsem.at[4 + i]) for i in range(2)]
    copies += [pltpu.make_async_copy(wp_hbm, wp, wsem.at[6])]
    for c in [load_wave, load_lens, weights[0], load_lens_v, weights[1]] + small + copies:
        c.start()

    blk[...] = jnp.zeros((512, 128), F32)
    load_wave.wait()
    wave = wave_v[0].astype(F32)
    for r in range(10):
        blk[pl.ds(r, 30, stride=16), :] = wave[:, 128 * r:128 * r + 128]
    blk[pl.ds(10, 29, stride=16), :] = wave[1:30, 0:128]
    blkb[...] = blk[...].astype(BF).reshape(32, 16, 128)

    load_lens.wait()

    mine_mod = residue(me)

    def tally(s, carry):
        total, mine, owners = carry[0], carry[1], carry[2:]
        mine = jnp.where(s == me, total, mine)
        total = total + lens_s[col, s]
        owners = tuple(o + jnp.where(total <= (mine_mod + NDP * j) * 1280, 1, 0) for j, o in enumerate(owners))
        return (total, mine) + owners
    zero = jnp.int32(0)
    counted = lax.fori_loop(0, NDP, tally, (zero,) * 18)
    start, owners = counted[1] // 1280, counted[2:]

    for t in range(NDP):
        send1[t] = blkb[(residue(t) - start) & 31]

    def centre(layer):
        copies[layer - 1].wait()
        ref, n, taps = (wm, layer - 1, 3) if layer <= 4 else (wl, layer - 5, 2)

        def one(i, c):
            at_row = pl.ds(pl.multiple_of(128 * (i & 3), 128), 128)
            v = ref[n, i >> 2, at_row, :].astype(F32)
            ref[n, i >> 2, at_row, :] = (v - jnp.sum(v, axis=-1, keepdims=True) * (1.0 / 512)).astype(BF)
            return c
        lax.fori_loop(0, 4 * taps, one, 0)

    def turn(g):
        weights[g].wait()
        pad = jnp.zeros((48, 128), F32)

        def one(ii, c):
            for u in range(4):
                i = 4 * ii + u
                wt[pl.ds(i, 128, stride=80), :] = jnp.concatenate([wraw[g, i].astype(F32), pad], axis=0).T
            return c
        lax.fori_loop(0, 20, one, 0)

        def pack(r, c):
            wb[g, pl.ds(pl.multiple_of(80 + r * 512, 16), 512), :] = wt[pl.ds(pl.multiple_of(r * 512, 512), 512), :].astype(BF)
            return c
        lax.fori_loop(0, 20, pack, 0)
        wb[g, 0:80, :] = jnp.zeros((80, 128), BF)
        wb[g, 10320:WROWS, :] = jnp.zeros((WROWS - 10320, 128), BF)
    centre(1)
    recv1[me] = send1[me]
    pl.semaphore_wait(barrier, len(greet))
    first = []
    for n, (dz, dy) in enumerate(steps):
        to = hop(dz, dy)
        c = pltpu.make_async_remote_copy(src_ref=send1.at[to], dst_ref=recv1.at[me], send_sem=s1.at[n],
                                         recv_sem=r1.at[n], device_id={"dp": to}, device_id_type=MESH)
        c.start()
        first.append(c)
    turn(0)
    for c in first:
        c.wait()
    half, slot = mine_mod >> 4, mine_mod & 15
    for j in range(16):
        send2[j] = recv1[jnp.minimum(owners[j], 31)]
    second = []
    for n in (4, 3, 5, 2, 6, 1, 7, 0):
        for m in range(2):
            j = (((me >> 2) + n) & 7) * 2 + m
            to = 2 * j + half
            c = pltpu.make_async_remote_copy(src_ref=send2.at[j], dst_ref=recv2.at[slot], send_sem=s2.at[j],
                                             recv_sem=r2.at[slot], device_id={"dp": to}, device_id_type=MESH)
            c.start()
            second.append(c)

    def spread(a, lo, hi):
        n = hi - lo + (1 if hi < 96 else 0)
        lane = lax.broadcasted_iota(jnp.int32, (8 * n, 128), 1)
        full = src[a, 16 * lo:16 * (lo + n + 1), :].reshape(n + 1, 2, 8, 128)
        ev, od = full[:, 0].reshape(8 * n + 8, 128), full[:, 1].reshape(8 * n + 8, 128)
        for par in range(2):
            f0 = (ev if par == 0 else od)[0:8 * n]
            f1 = od[0:8 * n] if par == 0 else ev[8:8 * n + 8]
            f2 = (ev if par == 0 else od)[8:8 * n + 8]
            t1 = pltpu.roll(f1, 80, 1)
            t2 = pltpu.roll(f2, 32, 1)
            v0 = jnp.where(lane < 80, f0, t1)
            v1 = jnp.where(lane < 32, t1, jnp.where(lane < 112, t2, 0.0))
            v = jnp.concatenate([v0, v1], axis=1)
            m = 8 * (hi - lo)
            x3[a, par, 0, 8 * lo:8 * lo + m, :] = v[0:m].astype(BF)
            k = m if hi < 96 else m - 16
            x3[a, par, 1, 8 * lo:8 * lo + k, :] = v[8:8 + k].astype(BF)

    row = lax.broadcasted_iota(jnp.int32, (NDP, 128), 0)
    lane = lax.broadcasted_iota(jnp.int32, (NDP, 128), 1)
    upper = jnp.where(row <= lane, 1.0, 0.0).astype(BF)
    load_lens_v.wait()
    ends = jnp.dot((lens_v[...].astype(F32) * (1.0 / 320)).astype(BF), upper, preferred_element_type=F32)
    ends = jnp.where(lax.broadcasted_iota(jnp.int32, (8, 128), 1) < NDP, ends, 1e9)
    frame = lax.broadcasted_iota(jnp.int32, (195, 8, 128), 0) + (64 * me - 64)
    past = jnp.where(ends[None] <= frame.astype(F32), 1.0, 0.0)
    clip = jnp.sum(past, axis=2, keepdims=True)
    here, after = clip[0:194], clip[1:195]
    ok = (here == after) & (frame[0:194, :, 0:1] >= 0) & (here < NDP)
    src[2, 0:1552, :] = jnp.broadcast_to(jnp.where(ok, here, -1.0), (194, 8, 128)).reshape(1552, 128)
    spread(2, 0, 96)
    for layer in range(2, 7):
        centre(layer)
    cc[...] = jnp.concatenate([src[2, 512:1024].reshape(32, 2, 8, 128)[:, 0].reshape(256, 128)] * 2, axis=1).astype(BF)
    for i in range(16):
        pltpu.make_async_remote_copy(src_ref=send2.at[0], dst_ref=recv2.at[i], send_sem=s2.at[0],
                                     recv_sem=r2.at[i], device_id={"dp": me}, device_id_type=MESH).wait_recv()
    for c in second:
        c.wait_send()

    rows[...] = recv2[...].astype(F32).reshape(256, 128)
    flat = jnp.concatenate([rows[pl.ds(r, 16, stride=16), :] for r in range(11)], axis=1)
    y = jnp.concatenate([flat[:, 160 * e:160 * e + 256] for e in range(8)], axis=0)
    xt[...] = y.T
    halo = jnp.broadcast_to(rows[250:251, :], (16, 128))
    line = lax.broadcasted_iota(jnp.int32, (16, 128), 0)
    xh = halo
    for p in range(1, 15):
        xh = jnp.where(line == p, pltpu.roll(halo, 128 - 5 * p, 1), xh)

    dn = (((0,), (0,)), ((), ()))
    for c in small:
        c.wait()
    gains, shifts = gain_v[...] * R2, shift_v[...] * R2
    g0, b0 = gains[0:1], shifts[0:1]
    w0 = w0_v[...].astype(F32)
    w0 = w0 - jnp.sum(w0, axis=-1, keepdims=True) * (1.0 / 512)
    w0 = jnp.concatenate([w0, jnp.zeros((6, 512), F32)], axis=0).astype(BF)

    def put(li, v):
        for t in range(4):
            hal[li, t, 0:v.shape[0], :] = v[:, 128 * t:128 * t + 128]

    def pick(li, begin, size, stride=1):
        ds = pl.ds(begin, size, stride=stride) if stride > 1 else pl.ds(begin, size)
        return jnp.concatenate([hal[li, t, ds, :] for t in range(4)], axis=1)

    h = jnp.dot(xh[:, 0:16].astype(BF), w0, preferred_element_type=F32)
    hal[...] = jnp.zeros(hal.shape, F32)
    put(0, norm_act(h, g0, b0, NORM_EPS))

    def l0(i, c):
        win = jnp.concatenate([xt[pl.ds(20 * i + 5 * q, 16), :] for q in range(4)], axis=1).astype(BF)
        h = lax.dot_general(win, w0, dn, preferred_element_type=F32)
        a = norm_act(h, g0, b0, NORM_EPS).astype(BF).reshape(4, 4, 2, 16, 512)
        for q in range(4):
            a0[4 * i + q] = a[q, :, 0].reshape(64, 512)
            a0[4 * i + q + 32] = a[q, :, 1].reshape(64, 512)
        return c
    lax.fori_loop(0, 8, l0, 0)

    srcs = [a0, a1, a2, a3, a4, a5]
    counts = [32, 16, 8, 4, 2, 1]
    for L in range(1, 7):
        inp, n = srcs[L - 1], counts[L - 1]
        K = 3 if L <= 4 else 2
        G = min(8, n)
        w = (lambda L=L: wm[L - 1].reshape(1536, 512)) if L <= 4 else (lambda L=L: wl[L - 5].reshape(1024, 512))
        g, s = gains[L:L + 1], shifts[L:L + 1]
        if K == 3:
            v = inp[0].astype(F32)
            inp[2 * n] = jnp.concatenate([v[16:64], v[1:16], pick(L - 1, 0, 1)], axis=0).astype(BF)

        def body(i, c, inp=inp, K=K, G=G, w=w, g=g, s=s, L=L, halo=False):
            taps = []
            for k in range(K):
                lhs = [inp[2 * (G * i + q) + k] for q in range(G)]
                if halo:
                    lhs.append(jnp.concatenate([pick(L - 1, k, 8, 2), jnp.zeros((8, 512), F32)], axis=0).astype(BF))
                taps.append(jnp.concatenate(lhs, axis=0) if len(lhs) > 1 else lhs[0])
            a = norm_act(jnp.dot(jnp.concatenate(taps, axis=1), w(), preferred_element_type=F32), g, s, 2 * NORM_EPS)
            if halo:
                put(L, a[64 * G:64 * G + 8])
            if L == 6:
                return a
            for q in range(G):
                srcs[L][G * i + q] = a[64 * q:64 * q + 64].astype(BF)
            return c
        last = body(0, 0, halo=(L <= 3))
        if n // G > 1:
            lax.fori_loop(1, n // G, body, 0)

    v = last.astype(BF).astype(F32)
    for t in range(4):
        for q in range(4):
            fr[t, pl.ds(q, 16, stride=4), :] = v[16 * q:16 * q + 16, 128 * t:128 * t + 128]
    v = jnp.concatenate([fr[t] for t in range(4)], axis=1)
    mean = jnp.sum(v, axis=-1, keepdims=True) * (1.0 / 512)
    cen = v - mean
    var = jnp.sum(cen * cen, axis=-1, keepdims=True) * (1.0 / 512)
    nf = (cen * lax.rsqrt(var + 2 * NORM_EPS) * pg_v[...] + ps_v[...]).astype(BF)
    copies[6].wait()
    pr = jnp.dot(nf, wp[...], preferred_element_type=F32) + jnp.concatenate([pb_v[r:r + 1, :] for r in range(10)], axis=1)
    for q in range(8):
        v = pr[:, 160 * q:160 * q + 160]
        rest = jnp.concatenate([v[16 * b:16 * b + 16, 128:160] for b in range(4)], axis=1)
        slab[q] = jnp.concatenate([v[:, 0:128], rest], axis=0).astype(BF)
    rcv[1, col] = slab[col]
    sends = []
    for n, (dr, dq) in enumerate(peers):
        to = at(dr, dq)
        c = pltpu.make_async_remote_copy(src_ref=slab.at[to["fsdp"]], dst_ref=rcv.at[1 - dr, col],
                                         send_sem=s3.at[n], recv_sem=r3.at[n], device_id=to, device_id_type=MESH)
        c.start()
        sends.append(c)

    flat = jnp.concatenate([kb_v[r:r + 1, :] for r in range(10)] + [jnp.zeros((1, 128), F32)], axis=1)
    bias = []
    for g in range(2):
        b = jnp.zeros((1, 128), F32)
        for q in range(NFS):
            b = jnp.where(col == q, flat[:, 160 * q + 80 * g:160 * q + 80 * g + 128], b)
        bias.append(b)
    turn(1)
    low = lax.broadcasted_iota(jnp.int32, (64, 128), 1) < 48

    def interleave(part):
        for c in range(NFS):
            v = rcv[part, c].astype(F32)
            rest = jnp.concatenate([pltpu.roll(v[64:80], (176 - 32 * b) & 127, 1) for b in range(4)], axis=0)
            src[0, pl.ds(512 * part + c, 64, stride=8), :] = v[0:64]
            src[1, pl.ds(512 * part + c, 64, stride=8), :] = jnp.where(low, pltpu.roll(v[0:64], 48, 1), rest)
    for g in range(2):
        src[g, 1536:1552, :] = jnp.zeros((16, 128), F32)
    for c in sends[0:15]:
        c.wait_recv()
    interleave(0)
    interleave(1)
    for g in range(2):
        spread(g, 0, 60)

    def taps(groups):
        def body(i, acc):
            ctr = cc[...]
            at_row = pl.multiple_of(48 * i, 16)
            tap = pl.multiple_of(960 * i, 16)
            masks = [x3[2, par, al, pl.ds(at_row + off, 256), :] == ctr for par, al, off in PLAN]
            out = []
            for n, g in enumerate(groups):
                lhs = jnp.concatenate([
                    jnp.where(m, x3[g, par, al, pl.ds(at_row + off, 256), :], jnp.zeros((), BF))
                    for m, (par, al, off) in zip(masks, PLAN)], axis=1)
                rhs = jnp.concatenate([
                    jnp.concatenate([wb[g, pl.ds(tap + 240 * s + 80, 256), :], wb[g, pl.ds(tap + 240 * s, 256), :]], axis=1)
                    for s in range(4)], axis=0)
                out.append(acc[n] + jnp.dot(lhs, rhs, preferred_element_type=F32))
            return tuple(out)
        return body
    acc = lax.fori_loop(0, 5, taps((0, 1)), (jnp.zeros((256, 256), F32),) * 2)
    part[...] = acc[1]
    for c in sends[15:23]:
        c.wait_recv()
    interleave(2)
    for g in range(2):
        spread(g, 60, 96)

    back = []
    for g in range(2):
        a = lax.fori_loop(5, 11, taps((g,)), ((acc[0] if g == 0 else part[...]),))[0]
        halves = []
        for v in range(2):
            pos = a[:, 128 * v:128 * v + 128] + bias[g]
            own = src[g, 512:1024].reshape(32, 2, 8, 128)[:, v].reshape(256, 128)
            mark = src[2, 512:1024].reshape(32, 2, 8, 128)[:, v].reshape(256, 128)
            gel = 0.5 * pos * (1.0 + lax.erf(pos * R2))
            halves.append(jnp.where(mark >= 0.0, own + gel, 0.0).reshape(32, 1, 8, 128))
        res[g] = jnp.concatenate(halves, axis=1).reshape(512, 128)
        for c in range(NFS):
            fin[g, c] = res[g, pl.ds(c, 64, stride=8), :].astype(BF)
        ret[g, col] = fin[g, col]
        for n, dq in enumerate((4, 5, 3, 6, 2, 7, 1)):
            to = at(0, dq)
            c = pltpu.make_async_remote_copy(src_ref=fin.at[g, to["fsdp"]], dst_ref=ret.at[g, col], send_sem=s4.at[g, n],
                                             recv_sem=r4.at[g, n], device_id=to, device_id_type=MESH)
            c.start()
            back.append(c)
    for c in sends:
        c.wait_send()
    for c in back:
        c.wait()
    out_ref[0] = jnp.concatenate([ret[g, q, :, 0:80] for q in range(NFS) for g in range(2)], axis=1)


def per_device(waveform, clip_lengths, conv_first, conv_mid, conv_last, conv_gain, conv_shift, proj_gain, proj_shift,
               proj_weight, proj_bias, pos_weight, pos_bias):
    H = pl.BlockSpec(memory_space=pltpu.HBM)
    D = pltpu.SemaphoreType.DMA
    V = pltpu.VMEM
    return pl.pallas_call(
        encoder_kernel,
        out_shape=jax.ShapeDtypeStruct((1, 64, 1280), BF),
        in_specs=[H] * 13,
        out_specs=pl.BlockSpec(memory_space=pltpu.VMEM),
        scratch_shapes=[V((1, 30, 1280), BF), pltpu.SMEM((8, 32), jnp.int32), V((8, 32), jnp.int32), V((10, 512), BF), V((7, 512), F32),
                        V((7, 512), F32), V((1, 512), F32), V((1, 512), F32), V((10, 128), F32), V((10, 128), F32),
                        V((512, 128), F32), V((32, 16, 128), BF), V((32, 16, 128), BF),
                        V((32, 16, 128), BF), V((16, 16, 128), BF), V((16, 16, 128), BF),
                        V((256, 128), F32), V((256, 128), F32),
                        V((65, 64, 512), BF), V((33, 64, 512), BF), V((17, 64, 512), BF),
                        V((9, 64, 512), BF), V((4, 64, 512), BF), V((2, 64, 512), BF),
                        V((4, 4, 24, 128), F32), V((4, 64, 128), F32),
                        V((4, 3, 512, 512), BF), V((2, 2, 512, 512), BF), V((512, 1280), BF),
                        V((8, 80, 128), BF), V((3, 8, 80, 128), BF), V((3, 1552, 128), F32), V((3, 2, 2, 768, 256), BF),
                        V((256, 256), BF), V((2, 80, 80, 128), BF), V((10240, 128), F32), V((2, WROWS, 128), BF), V((2, 512, 128), F32),
                        V((2, 8, 64, 128), BF), V((2, 8, 64, 128), BF), V((256, 256), F32),
                        D((9,)), D((10,)), D((32,)), D((32,)), D((16,)), D((16,)), D((23,)), D((23,)), D((2, 7)), D((2, 7))],
        compiler_params=pltpu.CompilerParams(vmem_limit_bytes=VMEM_MB << 20, collective_id=0, has_side_effects=True),
        name="encoder",
    )(waveform, clip_lengths[:, :, 0], conv_first, conv_mid, conv_last, conv_gain, conv_shift, proj_gain[None], proj_shift[None],
      proj_weight, proj_bias.reshape(10, 128), jnp.transpose(pos_weight, (0, 2, 3, 1)), pos_bias.reshape(10, 128))


def solution(mesh):
    return jax.shard_map(
        per_device,
        mesh=mesh,
        in_specs=(P("fsdp", "dp", None),) + (P(),) * 10 + (P("fsdp", None, None, None), P()),
        out_specs=P("fsdp", "dp", None),
        check_vma=False,
    )
```

```python
import jax
import jax.numpy as jnp
from jax import lax
from jax.experimental import pallas as pl
from jax.experimental.pallas import tpu as pltpu
from jax.sharding import PartitionSpec as P

NORM_EPS = 1e-5
R2 = 0.7071067811865476
F32, BF = jnp.float32, jnp.bfloat16
MESH = pl.DeviceIdType.MESH
NDP, NFS = 32, 8


def norm_act(h, gain, shift, eps):
    var = jnp.sum(h * h, axis=-1, keepdims=True) * (1.0 / h.shape[-1])
    z = h * lax.rsqrt(var + eps) * gain + shift
    return z + z * lax.erf(z)


VMEM_MB = 58
WROWS = 133 * 80 + 16
PLAN = ((0, 0, 0), (1, 1, 0), (0, 1, 16), (1, 0, 32))


def encoder_kernel(wave_hbm, lens_hbm, w0_hbm, wm_hbm, wl_hbm, gain_hbm, shift_hbm, pg_hbm, ps_hbm, wp_hbm, pb_hbm, wk_hbm,
                   kb_hbm, out_ref, wave_v, lens_s, lens_v, w0_v, gain_v, shift_v, pg_v, ps_v, pb_v, kb_v, blk, blkb, send1,
                   recv1, send2, recv2, rows, xt, a0, a1, a2, a3, a4, a5, hal, fr, wm, wl, wp, slab, rcv, src, x3, cc, wraw, wt,
                   wb, res, fin, ret, part, wsem, msem, s1, r1, s2, r2, s3, r3, s4, r4):
    me, col = lax.axis_index("dp"), lax.axis_index("fsdp")
    peers = [(dr, dq) for dr in (0, 1, -1) for dq in (4, 5, 3, 6, 2, 7, 1, 0) if (dr, dq) != (0, 0)]
    steps = sorted([(dz, dy) for dz in range(8) for dy in range(4) if dz or dy],
                   key=lambda s: -(min(s[0], 8 - s[0]) + min(s[1], 4 - s[1])))

    def at(dr, dq):
        return {"dp": (me + dr) & (NDP - 1), "fsdp": (col + dq) & (NFS - 1)}

    def hop(dz, dy):
        return (((me >> 2) + dz) & 7) * 4 + ((me + dy) & 3)

    def residue(d):
        return 16 * (1 - (d & 1)) + 2 * (d >> 2) + ((d & 3) >> 1)
    barrier = pltpu.get_barrier_semaphore()
    greet = [{"dp": hop(dz, dy)} for dz, dy in steps] + [at(dr, dq) for dr, dq in peers if dq]
    for to in greet:
        pl.semaphore_signal(barrier, inc=1, device_id=to, device_id_type=MESH)
    load_wave = pltpu.make_async_copy(wave_hbm, wave_v, msem.at[0])
    load_lens = pltpu.make_async_copy(lens_hbm, lens_s, msem.at[1])
    load_lens_v = pltpu.make_async_copy(lens_hbm, lens_v, msem.at[2])
    weights = [pltpu.make_async_copy(wk_hbm.at[g], wraw.at[g], wsem.at[7 + g]) for g in range(2)]
    pairs = ((w0_hbm, w0_v), (gain_hbm, gain_v), (shift_hbm, shift_v), (pg_hbm, pg_v), (ps_hbm, ps_v), (pb_hbm, pb_v), (kb_hbm, kb_v))
    small = [pltpu.make_async_copy(a, b, msem.at[3 + i]) for i, (a, b) in enumerate(pairs)]
    copies = [pltpu.make_async_copy(wm_hbm.at[i], wm.at[i], wsem.at[i]) for i in range(4)]
    copies += [pltpu.make_async_copy(wl_hbm.at[i], wl.at[i], wsem.at[4 + i]) for i in range(2)]
    copies += [pltpu.make_async_copy(wp_hbm, wp, wsem.at[6])]
    for c in [load_wave, load_lens, weights[0], load_lens_v, weights[1]] + small + copies:
        c.start()

    blk[...] = jnp.zeros((512, 128), F32)
    load_wave.wait()
    wave = wave_v[0].astype(F32)
    for r in range(10):
        blk[pl.ds(r, 30, stride=16), :] = wave[:, 128 * r:128 * r + 128]
    blk[pl.ds(10, 29, stride=16), :] = wave[1:30, 0:128]
    blkb[...] = blk[...].astype(BF).reshape(32, 16, 128)

    load_lens.wait()

    mine_mod = residue(me)

    def tally(s, carry):
        total, mine, owners = carry[0], carry[1], carry[2:]
        mine = jnp.where(s == me, total, mine)
        total = total + lens_s[col, s]
        owners = tuple(o + jnp.where(total <= (mine_mod + NDP * j) * 1280, 1, 0) for j, o in enumerate(owners))
        return (total, mine) + owners
    zero = jnp.int32(0)
    counted = lax.fori_loop(0, NDP, tally, (zero,) * 18)
    start, owners = counted[1] // 1280, counted[2:]

    for t in range(NDP):
        send1[t] = blkb[(residue(t) - start) & 31]

    def centre(layer):
        copies[layer - 1].wait()
        ref, n, taps = (wm, layer - 1, 3) if layer <= 4 else (wl, layer - 5, 2)

        def one(i, c):
            at_row = pl.ds(pl.multiple_of(128 * (i & 3), 128), 128)
            v = ref[n, i >> 2, at_row, :].astype(F32)
            ref[n, i >> 2, at_row, :] = (v - jnp.sum(v, axis=-1, keepdims=True) * (1.0 / 512)).astype(BF)
            return c
        lax.fori_loop(0, 4 * taps, one, 0)

    def turn(g):
        weights[g].wait()
        pad = jnp.zeros((48, 128), F32)

        def one(ii, c):
            for u in range(4):
                i = 4 * ii + u
                wt[pl.ds(i, 128, stride=80), :] = jnp.concatenate([wraw[g, i].astype(F32), pad], axis=0).T
            return c
        lax.fori_loop(0, 20, one, 0)

        def pack(r, c):
            wb[g, pl.ds(pl.multiple_of(80 + r * 512, 16), 512), :] = wt[pl.ds(pl.multiple_of(r * 512, 512), 512), :].astype(BF)
            return c
        lax.fori_loop(0, 20, pack, 0)
        wb[g, 0:80, :] = jnp.zeros((80, 128), BF)
        wb[g, 10320:WROWS, :] = jnp.zeros((WROWS - 10320, 128), BF)
    centre(1)
    recv1[me] = send1[me]
    pl.semaphore_wait(barrier, len(greet))
    first = []
    for n, (dz, dy) in enumerate(steps):
        to = hop(dz, dy)
        c = pltpu.make_async_remote_copy(src_ref=send1.at[to], dst_ref=recv1.at[me], send_sem=s1.at[n],
                                         recv_sem=r1.at[n], device_id={"dp": to}, device_id_type=MESH)
        c.start()
        first.append(c)
    turn(0)
    for c in first:
        c.wait()
    half, slot = mine_mod >> 4, mine_mod & 15
    for j in range(16):
        send2[j] = recv1[jnp.minimum(owners[j], 31)]
    second = []
    for n in (4, 3, 5, 2, 6, 1, 7, 0):
        for m in range(2):
            j = (((me >> 2) + n) & 7) * 2 + m
            to = 2 * j + half
            c = pltpu.make_async_remote_copy(src_ref=send2.at[j], dst_ref=recv2.at[slot], send_sem=s2.at[j],
                                             recv_sem=r2.at[slot], device_id={"dp": to}, device_id_type=MESH)
            c.start()
            second.append(c)

    def spread(a, lo, hi):
        n = hi - lo + (1 if hi < 96 else 0)
        lane = lax.broadcasted_iota(jnp.int32, (8 * n, 128), 1)
        full = src[a, 16 * lo:16 * (lo + n + 1), :].reshape(n + 1, 2, 8, 128)
        ev, od = full[:, 0].reshape(8 * n + 8, 128), full[:, 1].reshape(8 * n + 8, 128)
        for par in range(2):
            f0 = (ev if par == 0 else od)[0:8 * n]
            f1 = od[0:8 * n] if par == 0 else ev[8:8 * n + 8]
            f2 = (ev if par == 0 else od)[8:8 * n + 8]
            t1 = pltpu.roll(f1, 80, 1)
            t2 = pltpu.roll(f2, 32, 1)
            v0 = jnp.where(lane < 80, f0, t1)
            v1 = jnp.where(lane < 32, t1, jnp.where(lane < 112, t2, 0.0))
            v = jnp.concatenate([v0, v1], axis=1)
            m = 8 * (hi - lo)
            x3[a, par, 0, 8 * lo:8 * lo + m, :] = v[0:m].astype(BF)
            k = m if hi < 96 else m - 16
            x3[a, par, 1, 8 * lo:8 * lo + k, :] = v[8:8 + k].astype(BF)

    row = lax.broadcasted_iota(jnp.int32, (NDP, 128), 0)
    lane = lax.broadcasted_iota(jnp.int32, (NDP, 128), 1)
    upper = jnp.where(row <= lane, 1.0, 0.0).astype(BF)
    load_lens_v.wait()
    ends = jnp.dot((lens_v[...].astype(F32) * (1.0 / 320)).astype(BF), upper, preferred_element_type=F32)
    ends = jnp.where(lax.broadcasted_iota(jnp.int32, (8, 128), 1) < NDP, ends, 1e9)
    frame = lax.broadcasted_iota(jnp.int32, (195, 8, 128), 0) + (64 * me - 64)
    past = jnp.where(ends[None] <= frame.astype(F32), 1.0, 0.0)
    clip = jnp.sum(past, axis=2, keepdims=True)
    here, after = clip[0:194], clip[1:195]
    ok = (here == after) & (frame[0:194, :, 0:1] >= 0) & (here < NDP)
    src[2, 0:1552, :] = jnp.broadcast_to(jnp.where(ok, here, -1.0), (194, 8, 128)).reshape(1552, 128)
    spread(2, 0, 96)
    for layer in range(2, 7):
        centre(layer)
    cc[...] = jnp.concatenate([src[2, 512:1024].reshape(32, 2, 8, 128)[:, 0].reshape(256, 128)] * 2, axis=1).astype(BF)
    for i in range(16):
        pltpu.make_async_remote_copy(src_ref=send2.at[0], dst_ref=recv2.at[i], send_sem=s2.at[0],
                                     recv_sem=r2.at[i], device_id={"dp": me}, device_id_type=MESH).wait_recv()
    for c in second:
        c.wait_send()

    rows[...] = recv2[...].astype(F32).reshape(256, 128)
    flat = jnp.concatenate([rows[pl.ds(r, 16, stride=16), :] for r in range(11)], axis=1)
    y = jnp.concatenate([flat[:, 160 * e:160 * e + 256] for e in range(8)], axis=0)
    xt[...] = y.T
    halo = jnp.broadcast_to(rows[250:251, :], (16, 128))
    line = lax.broadcasted_iota(jnp.int32, (16, 128), 0)
    xh = halo
    for p in range(1, 15):
        xh = jnp.where(line == p, pltpu.roll(halo, 128 - 5 * p, 1), xh)

    dn = (((0,), (0,)), ((), ()))
    for c in small:
        c.wait()
    gains, shifts = gain_v[...] * R2, shift_v[...] * R2
    g0, b0 = gains[0:1], shifts[0:1]
    w0 = w0_v[...].astype(F32)
    w0 = w0 - jnp.sum(w0, axis=-1, keepdims=True) * (1.0 / 512)
    w0 = jnp.concatenate([w0, jnp.zeros((6, 512), F32)], axis=0).astype(BF)

    def put(li, v):
        for t in range(4):
            hal[li, t, 0:v.shape[0], :] = v[:, 128 * t:128 * t + 128]

    def pick(li, begin, size, stride=1):
        ds = pl.ds(begin, size, stride=stride) if stride > 1 else pl.ds(begin, size)
        return jnp.concatenate([hal[li, t, ds, :] for t in range(4)], axis=1)

    h = jnp.dot(xh[:, 0:16].astype(BF), w0, preferred_element_type=F32)
    hal[...] = jnp.zeros(hal.shape, F32)
    put(0, norm_act(h, g0, b0, NORM_EPS))

    def l0(i, c):
        win = jnp.concatenate([xt[pl.ds(20 * i + 5 * q, 16), :] for q in range(4)], axis=1).astype(BF)
        h = lax.dot_general(win, w0, dn, preferred_element_type=F32)
        a = norm_act(h, g0, b0, NORM_EPS).astype(BF).reshape(4, 4, 2, 16, 512)
        for q in range(4):
            a0[4 * i + q] = a[q, :, 0].reshape(64, 512)
            a0[4 * i + q + 32] = a[q, :, 1].reshape(64, 512)
        return c
    lax.fori_loop(0, 8, l0, 0, unroll=True)

    srcs = [a0, a1, a2, a3, a4, a5]
    counts = [32, 16, 8, 4, 2, 1]
    for L in range(1, 7):
        inp, n = srcs[L - 1], counts[L - 1]
        K = 3 if L <= 4 else 2
        G = min(8, n)
        w = (lambda L=L: wm[L - 1].reshape(1536, 512)) if L <= 4 else (lambda L=L: wl[L - 5].reshape(1024, 512))
        g, s = gains[L:L + 1], shifts[L:L + 1]
        if K == 3:
            v = inp[0].astype(F32)
            inp[2 * n] = jnp.concatenate([v[16:64], v[1:16], pick(L - 1, 0, 1)], axis=0).astype(BF)

        def body(i, c, inp=inp, K=K, G=G, w=w, g=g, s=s, L=L, halo=False):
            taps = []
            for k in range(K):
                lhs = [inp[2 * (G * i + q) + k] for q in range(G)]
                if halo:
                    lhs.append(jnp.concatenate([pick(L - 1, k, 8, 2), jnp.zeros((8, 512), F32)], axis=0).astype(BF))
                taps.append(jnp.concatenate(lhs, axis=0) if len(lhs) > 1 else lhs[0])
            a = norm_act(jnp.dot(jnp.concatenate(taps, axis=1), w(), preferred_element_type=F32), g, s, 2 * NORM_EPS)
            if halo:
                put(L, a[64 * G:64 * G + 8])
            if L == 6:
                return a
            for q in range(G):
                srcs[L][G * i + q] = a[64 * q:64 * q + 64].astype(BF)
            return c
        last = body(0, 0, halo=(L <= 3))
        if n // G > 1:
            lax.fori_loop(1, n // G, body, 0, unroll=True)

    v = last.astype(BF).astype(F32)
    for t in range(4):
        for q in range(4):
            fr[t, pl.ds(q, 16, stride=4), :] = v[16 * q:16 * q + 16, 128 * t:128 * t + 128]
    v = jnp.concatenate([fr[t] for t in range(4)], axis=1)
    mean = jnp.sum(v, axis=-1, keepdims=True) * (1.0 / 512)
    cen = v - mean
    var = jnp.sum(cen * cen, axis=-1, keepdims=True) * (1.0 / 512)
    nf = (cen * lax.rsqrt(var + 2 * NORM_EPS) * pg_v[...] + ps_v[...]).astype(BF)
    copies[6].wait()
    pr = jnp.dot(nf, wp[...], preferred_element_type=F32) + jnp.concatenate([pb_v[r:r + 1, :] for r in range(10)], axis=1)
    for q in range(8):
        v = pr[:, 160 * q:160 * q + 160]
        rest = jnp.concatenate([v[16 * b:16 * b + 16, 128:160] for b in range(4)], axis=1)
        slab[q] = jnp.concatenate([v[:, 0:128], rest], axis=0).astype(BF)
    rcv[1, col] = slab[col]
    sends = []
    for n, (dr, dq) in enumerate(peers):
        to = at(dr, dq)
        c = pltpu.make_async_remote_copy(src_ref=slab.at[to["fsdp"]], dst_ref=rcv.at[1 - dr, col],
                                         send_sem=s3.at[n], recv_sem=r3.at[n], device_id=to, device_id_type=MESH)
        c.start()
        sends.append(c)

    flat = jnp.concatenate([kb_v[r:r + 1, :] for r in range(10)] + [jnp.zeros((1, 128), F32)], axis=1)
    bias = []
    for g in range(2):
        b = jnp.zeros((1, 128), F32)
        for q in range(NFS):
            b = jnp.where(col == q, flat[:, 160 * q + 80 * g:160 * q + 80 * g + 128], b)
        bias.append(b)
    turn(1)
    low = lax.broadcasted_iota(jnp.int32, (64, 128), 1) < 48

    def interleave(part):
        for c in range(NFS):
            v = rcv[part, c].astype(F32)
            rest = jnp.concatenate([pltpu.roll(v[64:80], (176 - 32 * b) & 127, 1) for b in range(4)], axis=0)
            src[0, pl.ds(512 * part + c, 64, stride=8), :] = v[0:64]
            src[1, pl.ds(512 * part + c, 64, stride=8), :] = jnp.where(low, pltpu.roll(v[0:64], 48, 1), rest)
    for g in range(2):
        src[g, 1536:1552, :] = jnp.zeros((16, 128), F32)
    for c in sends[0:15]:
        c.wait_recv()
    interleave(0)
    interleave(1)
    for g in range(2):
        spread(g, 0, 60)

    def taps(groups):
        def body(i, acc):
            ctr = cc[...]
            at_row = pl.multiple_of(48 * i, 16)
            tap = pl.multiple_of(960 * i, 16)
            masks = [x3[2, par, al, pl.ds(at_row + off, 256), :] == ctr for par, al, off in PLAN]
            out = []
            for n, g in enumerate(groups):
                lhs = jnp.concatenate([
                    jnp.where(m, x3[g, par, al, pl.ds(at_row + off, 256), :], jnp.zeros((), BF))
                    for m, (par, al, off) in zip(masks, PLAN)], axis=1)
                rhs = jnp.concatenate([
                    jnp.concatenate([wb[g, pl.ds(tap + 240 * s + 80, 256), :], wb[g, pl.ds(tap + 240 * s, 256), :]], axis=1)
                    for s in range(4)], axis=0)
                out.append(acc[n] + jnp.dot(lhs, rhs, preferred_element_type=F32))
            return tuple(out)
        return body
    acc = lax.fori_loop(0, 5, taps((0, 1)), (jnp.zeros((256, 256), F32),) * 2, unroll=True)
    part[...] = acc[1]
    for c in sends[15:23]:
        c.wait_recv()
    interleave(2)
    for g in range(2):
        spread(g, 60, 96)

    back = []
    for g in range(2):
        a = lax.fori_loop(5, 11, taps((g,)), ((acc[0] if g == 0 else part[...]),), unroll=True)[0]
        halves = []
        for v in range(2):
            pos = a[:, 128 * v:128 * v + 128] + bias[g]
            own = src[g, 512:1024].reshape(32, 2, 8, 128)[:, v].reshape(256, 128)
            mark = src[2, 512:1024].reshape(32, 2, 8, 128)[:, v].reshape(256, 128)
            gel = 0.5 * pos * (1.0 + lax.erf(pos * R2))
            halves.append(jnp.where(mark >= 0.0, own + gel, 0.0).reshape(32, 1, 8, 128))
        res[g] = jnp.concatenate(halves, axis=1).reshape(512, 128)
        for c in range(NFS):
            fin[g, c] = res[g, pl.ds(c, 64, stride=8), :].astype(BF)
        ret[g, col] = fin[g, col]
        for n, dq in enumerate((4, 5, 3, 6, 2, 7, 1)):
            to = at(0, dq)
            c = pltpu.make_async_remote_copy(src_ref=fin.at[g, to["fsdp"]], dst_ref=ret.at[g, col], send_sem=s4.at[g, n],
                                             recv_sem=r4.at[g, n], device_id=to, device_id_type=MESH)
            c.start()
            back.append(c)
    for c in sends:
        c.wait_send()
    for c in back:
        c.wait()
    out_ref[0] = jnp.concatenate([ret[g, q, :, 0:80] for q in range(NFS) for g in range(2)], axis=1)


def per_device(waveform, clip_lengths, conv_first, conv_mid, conv_last, conv_gain, conv_shift, proj_gain, proj_shift,
               proj_weight, proj_bias, pos_weight, pos_bias):
    H = pl.BlockSpec(memory_space=pltpu.HBM)
    D = pltpu.SemaphoreType.DMA
    V = pltpu.VMEM
    return pl.pallas_call(
        encoder_kernel,
        out_shape=jax.ShapeDtypeStruct((1, 64, 1280), BF),
        in_specs=[H] * 13,
        out_specs=pl.BlockSpec(memory_space=pltpu.VMEM),
        scratch_shapes=[V((1, 30, 1280), BF), pltpu.SMEM((8, 32), jnp.int32), V((8, 32), jnp.int32), V((10, 512), BF), V((7, 512), F32),
                        V((7, 512), F32), V((1, 512), F32), V((1, 512), F32), V((10, 128), F32), V((10, 128), F32),
                        V((512, 128), F32), V((32, 16, 128), BF), V((32, 16, 128), BF),
                        V((32, 16, 128), BF), V((16, 16, 128), BF), V((16, 16, 128), BF),
                        V((256, 128), F32), V((256, 128), F32),
                        V((65, 64, 512), BF), V((33, 64, 512), BF), V((17, 64, 512), BF),
                        V((9, 64, 512), BF), V((4, 64, 512), BF), V((2, 64, 512), BF),
                        V((4, 4, 24, 128), F32), V((4, 64, 128), F32),
                        V((4, 3, 512, 512), BF), V((2, 2, 512, 512), BF), V((512, 1280), BF),
                        V((8, 80, 128), BF), V((3, 8, 80, 128), BF), V((3, 1552, 128), F32), V((3, 2, 2, 768, 256), BF),
                        V((256, 256), BF), V((2, 80, 80, 128), BF), V((10240, 128), F32), V((2, WROWS, 128), BF), V((2, 512, 128), F32),
                        V((2, 8, 64, 128), BF), V((2, 8, 64, 128), BF), V((256, 256), F32),
                        D((9,)), D((10,)), D((32,)), D((32,)), D((16,)), D((16,)), D((23,)), D((23,)), D((2, 7)), D((2, 7))],
        compiler_params=pltpu.CompilerParams(vmem_limit_bytes=VMEM_MB << 20, collective_id=0, has_side_effects=True),
        name="encoder",
    )(waveform, clip_lengths[:, :, 0], conv_first, conv_mid, conv_last, conv_gain, conv_shift, proj_gain[None], proj_shift[None],
      proj_weight, proj_bias.reshape(10, 128), jnp.transpose(pos_weight, (0, 2, 3, 1)), pos_bias.reshape(10, 128))


def solution(mesh):
    return jax.shard_map(
        per_device,
        mesh=mesh,
        in_specs=(P("fsdp", "dp", None),) + (P(),) * 10 + (P("fsdp", None, None, None), P()),
        out_specs=P("fsdp", "dp", None),
        check_vma=False,
    )
```

```python
import jax
import jax.numpy as jnp
from jax import lax
from jax.experimental import pallas as pl
from jax.experimental.pallas import tpu as pltpu
from jax.sharding import PartitionSpec as P

NORM_EPS = 1e-5
R2 = 0.7071067811865476
F32, BF = jnp.float32, jnp.bfloat16
MESH = pl.DeviceIdType.MESH
NDP, NFS = 32, 8


def norm_act(h, gain, shift, eps):
    var = jnp.sum(h * h, axis=-1, keepdims=True) * (1.0 / h.shape[-1])
    z = h * lax.rsqrt(var + eps) * gain + shift
    return z + z * lax.erf(z)


VMEM_MB = 58
WROWS = 133 * 80 + 16
PLAN = ((0, 0, 0), (1, 1, 0), (0, 1, 16), (1, 0, 32))


def encoder_kernel(wave_hbm, lens_hbm, w0_hbm, wm_hbm, wl_hbm, gain_hbm, shift_hbm, pg_hbm, ps_hbm, wp_hbm, pb_hbm, wk_hbm,
                   kb_hbm, out_ref, wave_v, lens_s, lens_v, w0_v, gain_v, shift_v, pg_v, ps_v, pb_v, kb_v, blk, blkb, send1,
                   recv1, send2, recv2, rows, xt, a0, a1, a2, a3, a4, a5, hal, fr, wm, wl, wp, slab, rcv, src, x3, cc, wraw, wt,
                   wb, res, fin, ret, part, wsem, msem, s1, r1, s2, r2, s3, r3, s4, r4):
    me, col = lax.axis_index("dp"), lax.axis_index("fsdp")
    peers = [(dr, dq) for dr in (0, 1, -1) for dq in (4, 5, 3, 6, 2, 7, 1, 0) if (dr, dq) != (0, 0)]
    steps = sorted([(dz, dy) for dz in range(8) for dy in range(4) if dz or dy],
                   key=lambda s: -(min(s[0], 8 - s[0]) + min(s[1], 4 - s[1])))

    def at(dr, dq):
        return {"dp": (me + dr) & (NDP - 1), "fsdp": (col + dq) & (NFS - 1)}

    def hop(dz, dy):
        return (((me >> 2) + dz) & 7) * 4 + ((me + dy) & 3)

    def residue(d):
        return 16 * (1 - (d & 1)) + 2 * (d >> 2) + ((d & 3) >> 1)
    barrier = pltpu.get_barrier_semaphore()
    greet = [{"dp": hop(dz, dy)} for dz, dy in steps] + [at(dr, dq) for dr, dq in peers if dq]
    for to in greet:
        pl.semaphore_signal(barrier, inc=1, device_id=to, device_id_type=MESH)
    load_wave = pltpu.make_async_copy(wave_hbm, wave_v, msem.at[0])
    load_lens = pltpu.make_async_copy(lens_hbm, lens_s, msem.at[1])
    load_lens_v = pltpu.make_async_copy(lens_hbm, lens_v, msem.at[2])
    weights = [pltpu.make_async_copy(wk_hbm.at[g], wraw.at[g], wsem.at[7 + g]) for g in range(2)]
    pairs = ((w0_hbm, w0_v), (gain_hbm, gain_v), (shift_hbm, shift_v), (pg_hbm, pg_v), (ps_hbm, ps_v), (pb_hbm, pb_v), (kb_hbm, kb_v))
    small = [pltpu.make_async_copy(a, b, msem.at[3 + i]) for i, (a, b) in enumerate(pairs)]
    copies = [pltpu.make_async_copy(wm_hbm.at[i], wm.at[i], wsem.at[i]) for i in range(4)]
    copies += [pltpu.make_async_copy(wl_hbm.at[i], wl.at[i], wsem.at[4 + i]) for i in range(2)]
    copies += [pltpu.make_async_copy(wp_hbm, wp, wsem.at[6])]
    for c in [load_wave, load_lens, weights[0], load_lens_v, weights[1]] + small + copies:
        c.start()

    blk[...] = jnp.zeros((512, 128), F32)
    load_wave.wait()
    wave = wave_v[0].astype(F32)
    for r in range(10):
        blk[pl.ds(r, 30, stride=16), :] = wave[:, 128 * r:128 * r + 128]
    blk[pl.ds(10, 29, stride=16), :] = wave[1:30, 0:128]
    blkb[...] = blk[...].astype(BF).reshape(32, 16, 128)

    load_lens.wait()

    mine_mod = residue(me)

    def tally(s, carry):
        total, mine, owners = carry[0], carry[1], carry[2:]
        mine = jnp.where(s == me, total, mine)
        total = total + lens_s[col, s]
        owners = tuple(o + jnp.where(total <= (mine_mod + NDP * j) * 1280, 1, 0) for j, o in enumerate(owners))
        return (total, mine) + owners
    zero = jnp.int32(0)
    counted = lax.fori_loop(0, NDP, tally, (zero,) * 18)
    start, owners = counted[1] // 1280, counted[2:]

    for t in range(NDP):
        send1[t] = blkb[(residue(t) - start) & 31]

    def centre(layer):
        copies[layer - 1].wait()
        ref, n, taps = (wm, layer - 1, 3) if layer <= 4 else (wl, layer - 5, 2)

        def one(i, c):
            at_row = pl.ds(pl.multiple_of(128 * (i & 3), 128), 128)
            v = ref[n, i >> 2, at_row, :].astype(F32)
            ref[n, i >> 2, at_row, :] = (v - jnp.sum(v, axis=-1, keepdims=True) * (1.0 / 512)).astype(BF)
            return c
        lax.fori_loop(0, 4 * taps, one, 0)

    def turn(g):
        weights[g].wait()
        pad = jnp.zeros((48, 128), F32)

        def one(ii, c):
            for u in range(4):
                i = 4 * ii + u
                wt[pl.ds(i, 128, stride=80), :] = jnp.concatenate([wraw[g, i].astype(F32), pad], axis=0).T
            return c
        lax.fori_loop(0, 20, one, 0)

        def pack(r, c):
            wb[g, pl.ds(pl.multiple_of(80 + r * 512, 16), 512), :] = wt[pl.ds(pl.multiple_of(r * 512, 512), 512), :].astype(BF)
            return c
        lax.fori_loop(0, 20, pack, 0)
        wb[g, 0:80, :] = jnp.zeros((80, 128), BF)
        wb[g, 10320:WROWS, :] = jnp.zeros((WROWS - 10320, 128), BF)
    centre(1)
    recv1[me] = send1[me]
    pl.semaphore_wait(barrier, len(greet))
    first = []
    for n, (dz, dy) in enumerate(steps):
        to = hop(dz, dy)
        c = pltpu.make_async_remote_copy(src_ref=send1.at[to], dst_ref=recv1.at[me], send_sem=s1.at[n],
                                         recv_sem=r1.at[n], device_id={"dp": to}, device_id_type=MESH)
        c.start()
        first.append(c)
    turn(0)
    for c in first:
        c.wait()
    half, slot = mine_mod >> 4, mine_mod & 15
    for j in range(16):
        send2[j] = recv1[jnp.minimum(owners[j], 31)]
    second = []
    for n in (4, 3, 5, 2, 6, 1, 7, 0):
        for m in range(2):
            j = (((me >> 2) + n) & 7) * 2 + m
            to = 2 * j + half
            c = pltpu.make_async_remote_copy(src_ref=send2.at[j], dst_ref=recv2.at[slot], send_sem=s2.at[j],
                                             recv_sem=r2.at[slot], device_id={"dp": to}, device_id_type=MESH)
            c.start()
            second.append(c)

    def spread(a, lo, hi):
        n = hi - lo + (1 if hi < 96 else 0)
        lane = lax.broadcasted_iota(jnp.int32, (8 * n, 128), 1)
        full = src[a, 16 * lo:16 * (lo + n + 1), :].reshape(n + 1, 2, 8, 128)
        ev, od = full[:, 0].reshape(8 * n + 8, 128), full[:, 1].reshape(8 * n + 8, 128)
        for par in range(2):
            f0 = (ev if par == 0 else od)[0:8 * n]
            f1 = od[0:8 * n] if par == 0 else ev[8:8 * n + 8]
            f2 = (ev if par == 0 else od)[8:8 * n + 8]
            t1 = pltpu.roll(f1, 80, 1)
            t2 = pltpu.roll(f2, 32, 1)
            v0 = jnp.where(lane < 80, f0, t1)
            v1 = jnp.where(lane < 32, t1, jnp.where(lane < 112, t2, 0.0))
            v = jnp.concatenate([v0, v1], axis=1)
            m = 8 * (hi - lo)
            x3[a, par, 0, 8 * lo:8 * lo + m, :] = v[0:m].astype(BF)
            k = m if hi < 96 else m - 16
            x3[a, par, 1, 8 * lo:8 * lo + k, :] = v[8:8 + k].astype(BF)

    row = lax.broadcasted_iota(jnp.int32, (NDP, 128), 0)
    lane = lax.broadcasted_iota(jnp.int32, (NDP, 128), 1)
    upper = jnp.where(row <= lane, 1.0, 0.0).astype(BF)
    load_lens_v.wait()
    ends = jnp.dot((lens_v[...].astype(F32) * (1.0 / 320)).astype(BF), upper, preferred_element_type=F32)
    ends = jnp.where(lax.broadcasted_iota(jnp.int32, (8, 128), 1) < NDP, ends, 1e9)
    frame = lax.broadcasted_iota(jnp.int32, (195, 8, 128), 0) + (64 * me - 64)
    past = jnp.where(ends[None] <= frame.astype(F32), 1.0, 0.0)
    clip = jnp.sum(past, axis=2, keepdims=True)
    here, after = clip[0:194], clip[1:195]
    ok = (here == after) & (frame[0:194, :, 0:1] >= 0) & (here < NDP)
    src[2, 0:1552, :] = jnp.broadcast_to(jnp.where(ok, here, -1.0), (194, 8, 128)).reshape(1552, 128)
    spread(2, 0, 96)
    for layer in range(2, 7):
        centre(layer)
    cc[...] = jnp.concatenate([src[2, 512:1024].reshape(32, 2, 8, 128)[:, 0].reshape(256, 128)] * 2, axis=1).astype(BF)
    for i in range(16):
        pltpu.make_async_remote_copy(src_ref=send2.at[0], dst_ref=recv2.at[i], send_sem=s2.at[0],
                                     recv_sem=r2.at[i], device_id={"dp": me}, device_id_type=MESH).wait_recv()
    for c in second:
        c.wait_send()

    rows[...] = recv2[...].astype(F32).reshape(256, 128)
    flat = jnp.concatenate([rows[pl.ds(r, 16, stride=16), :] for r in range(11)], axis=1)
    y = jnp.concatenate([flat[:, 160 * e:160 * e + 256] for e in range(8)], axis=0)
    xt[...] = y.T
    halo = jnp.broadcast_to(rows[250:251, :], (16, 128))
    line = lax.broadcasted_iota(jnp.int32, (16, 128), 0)
    xh = halo
    for p in range(1, 15):
        xh = jnp.where(line == p, pltpu.roll(halo, 128 - 5 * p, 1), xh)

    dn = (((0,), (0,)), ((), ()))
    for c in small:
        c.wait()
    gains, shifts = gain_v[...] * R2, shift_v[...] * R2
    g0, b0 = gains[0:1], shifts[0:1]
    w0 = w0_v[...].astype(F32)
    w0 = w0 - jnp.sum(w0, axis=-1, keepdims=True) * (1.0 / 512)
    w0 = jnp.concatenate([w0, jnp.zeros((6, 512), F32)], axis=0).astype(BF)

    def put(li, v):
        for t in range(4):
            hal[li, t, 0:v.shape[0], :] = v[:, 128 * t:128 * t + 128]

    def pick(li, begin, size, stride=1):
        ds = pl.ds(begin, size, stride=stride) if stride > 1 else pl.ds(begin, size)
        return jnp.concatenate([hal[li, t, ds, :] for t in range(4)], axis=1)

    h = jnp.dot(xh[:, 0:16].astype(BF), w0, preferred_element_type=F32)
    hal[...] = jnp.zeros(hal.shape, F32)
    put(0, norm_act(h, g0, b0, NORM_EPS))

    def l0(i, c):
        win = jnp.concatenate([xt[pl.ds(20 * i + 5 * q, 16), :] for q in range(4)], axis=1).astype(BF)
        h = lax.dot_general(win, w0, dn, preferred_element_type=F32)
        a = norm_act(h, g0, b0, NORM_EPS).astype(BF).reshape(4, 4, 2, 16, 512)
        for q in range(4):
            a0[4 * i + q] = a[q, :, 0].reshape(64, 512)
            a0[4 * i + q + 32] = a[q, :, 1].reshape(64, 512)
        return c
    lax.fori_loop(0, 8, l0, 0, unroll=True)

    srcs = [a0, a1, a2, a3, a4, a5]
    counts = [32, 16, 8, 4, 2, 1]
    for L in range(1, 7):
        inp, n = srcs[L - 1], counts[L - 1]
        K = 3 if L <= 4 else 2
        G = min(8, n)
        w = (lambda L=L: wm[L - 1].reshape(1536, 512)) if L <= 4 else (lambda L=L: wl[L - 5].reshape(1024, 512))
        g, s = gains[L:L + 1], shifts[L:L + 1]
        if K == 3:
            v = inp[0].astype(F32)
            inp[2 * n] = jnp.concatenate([v[16:64], v[1:16], pick(L - 1, 0, 1)], axis=0).astype(BF)

        def body(i, c, inp=inp, K=K, G=G, w=w, g=g, s=s, L=L, halo=False):
            taps = []
            for k in range(K):
                lhs = [inp[2 * (G * i + q) + k] for q in range(G)]
                if halo:
                    lhs.append(jnp.concatenate([pick(L - 1, k, 8, 2), jnp.zeros((8, 512), F32)], axis=0).astype(BF))
                taps.append(jnp.concatenate(lhs, axis=0) if len(lhs) > 1 else lhs[0])
            a = norm_act(jnp.dot(jnp.concatenate(taps, axis=1), w(), preferred_element_type=F32), g, s, 2 * NORM_EPS)
            if halo:
                put(L, a[64 * G:64 * G + 8])
            if L == 6:
                return a
            for q in range(G):
                srcs[L][G * i + q] = a[64 * q:64 * q + 64].astype(BF)
            return c
        last = body(0, 0, halo=(L <= 3))
        if n // G > 1:
            lax.fori_loop(1, n // G, body, 0, unroll=True)

    v = last.astype(BF).astype(F32)
    for t in range(4):
        for q in range(4):
            fr[t, pl.ds(q, 16, stride=4), :] = v[16 * q:16 * q + 16, 128 * t:128 * t + 128]
    v = jnp.concatenate([fr[t] for t in range(4)], axis=1)
    mean = jnp.sum(v, axis=-1, keepdims=True) * (1.0 / 512)
    cen = v - mean
    var = jnp.sum(cen * cen, axis=-1, keepdims=True) * (1.0 / 512)
    nf = (cen * lax.rsqrt(var + 2 * NORM_EPS) * pg_v[...] + ps_v[...]).astype(BF)
    copies[6].wait()
    pr = jnp.dot(nf, wp[...], preferred_element_type=F32) + jnp.concatenate([pb_v[r:r + 1, :] for r in range(10)], axis=1)
    for q in range(8):
        v = pr[:, 160 * q:160 * q + 160]
        rest = jnp.concatenate([v[16 * b:16 * b + 16, 128:160] for b in range(4)], axis=1)
        slab[q] = jnp.concatenate([v[:, 0:128], rest], axis=0).astype(BF)
    rcv[1, col] = slab[col]
    sends = []
    for n, (dr, dq) in enumerate(peers):
        to = at(dr, dq)
        c = pltpu.make_async_remote_copy(src_ref=slab.at[to["fsdp"]], dst_ref=rcv.at[1 - dr, col],
                                         send_sem=s3.at[n], recv_sem=r3.at[n], device_id=to, device_id_type=MESH)
        c.start()
        sends.append(c)

    flat = jnp.concatenate([kb_v[r:r + 1, :] for r in range(10)] + [jnp.zeros((1, 128), F32)], axis=1)
    bias = []
    for g in range(2):
        b = jnp.zeros((1, 128), F32)
        for q in range(NFS):
            b = jnp.where(col == q, flat[:, 160 * q + 80 * g:160 * q + 80 * g + 128], b)
        bias.append(b)
    turn(1)
    low = lax.broadcasted_iota(jnp.int32, (64, 128), 1) < 48

    def interleave(part):
        for c in range(NFS):
            v = rcv[part, c].astype(F32)
            rest = jnp.concatenate([pltpu.roll(v[64:80], (176 - 32 * b) & 127, 1) for b in range(4)], axis=0)
            src[0, pl.ds(512 * part + c, 64, stride=8), :] = v[0:64]
            src[1, pl.ds(512 * part + c, 64, stride=8), :] = jnp.where(low, pltpu.roll(v[0:64], 48, 1), rest)
    for g in range(2):
        src[g, 1536:1552, :] = jnp.zeros((16, 128), F32)
    for c in sends[0:7]:
        c.wait_recv()
    interleave(1)
    for g in range(2):
        spread(g, 32, 60)
    for c in sends[7:15]:
        c.wait_recv()
    interleave(0)
    for g in range(2):
        spread(g, 0, 32)

    def taps(groups):
        def body(i, acc):
            ctr = cc[...]
            at_row = pl.multiple_of(48 * i, 16)
            tap = pl.multiple_of(960 * i, 16)
            masks = [x3[2, par, al, pl.ds(at_row + off, 256), :] == ctr for par, al, off in PLAN]
            out = []
            for n, g in enumerate(groups):
                lhs = jnp.concatenate([
                    jnp.where(m, x3[g, par, al, pl.ds(at_row + off, 256), :], jnp.zeros((), BF))
                    for m, (par, al, off) in zip(masks, PLAN)], axis=1)
                rhs = jnp.concatenate([
                    jnp.concatenate([wb[g, pl.ds(tap + 240 * s + 80, 256), :], wb[g, pl.ds(tap + 240 * s, 256), :]], axis=1)
                    for s in range(4)], axis=0)
                out.append(acc[n] + jnp.dot(lhs, rhs, preferred_element_type=F32))
            return tuple(out)
        return body
    acc = lax.fori_loop(0, 5, taps((0, 1)), (jnp.zeros((256, 256), F32),) * 2, unroll=True)
    part[...] = acc[1]
    for c in sends[15:23]:
        c.wait_recv()
    interleave(2)
    for g in range(2):
        spread(g, 60, 96)

    back = []
    for g in range(2):
        a = lax.fori_loop(5, 11, taps((g,)), ((acc[0] if g == 0 else part[...]),), unroll=True)[0]
        halves = []
        for v in range(2):
            pos = a[:, 128 * v:128 * v + 128] + bias[g]
            own = src[g, 512:1024].reshape(32, 2, 8, 128)[:, v].reshape(256, 128)
            mark = src[2, 512:1024].reshape(32, 2, 8, 128)[:, v].reshape(256, 128)
            gel = 0.5 * pos * (1.0 + lax.erf(pos * R2))
            halves.append(jnp.where(mark >= 0.0, own + gel, 0.0).reshape(32, 1, 8, 128))
        res[g] = jnp.concatenate(halves, axis=1).reshape(512, 128)
        for c in range(NFS):
            fin[g, c] = res[g, pl.ds(c, 64, stride=8), :].astype(BF)
        ret[g, col] = fin[g, col]
        for n, dq in enumerate((4, 5, 3, 6, 2, 7, 1)):
            to = at(0, dq)
            c = pltpu.make_async_remote_copy(src_ref=fin.at[g, to["fsdp"]], dst_ref=ret.at[g, col], send_sem=s4.at[g, n],
                                             recv_sem=r4.at[g, n], device_id=to, device_id_type=MESH)
            c.start()
            back.append(c)
    for c in sends:
        c.wait_send()
    for c in back:
        c.wait()
    out_ref[0] = jnp.concatenate([ret[g, q, :, 0:80] for q in range(NFS) for g in range(2)], axis=1)


def per_device(waveform, clip_lengths, conv_first, conv_mid, conv_last, conv_gain, conv_shift, proj_gain, proj_shift,
               proj_weight, proj_bias, pos_weight, pos_bias):
    H = pl.BlockSpec(memory_space=pltpu.HBM)
    D = pltpu.SemaphoreType.DMA
    V = pltpu.VMEM
    return pl.pallas_call(
        encoder_kernel,
        out_shape=jax.ShapeDtypeStruct((1, 64, 1280), BF),
        in_specs=[H] * 13,
        out_specs=pl.BlockSpec(memory_space=pltpu.VMEM),
        scratch_shapes=[V((1, 30, 1280), BF), pltpu.SMEM((8, 32), jnp.int32), V((8, 32), jnp.int32), V((10, 512), BF), V((7, 512), F32),
                        V((7, 512), F32), V((1, 512), F32), V((1, 512), F32), V((10, 128), F32), V((10, 128), F32),
                        V((512, 128), F32), V((32, 16, 128), BF), V((32, 16, 128), BF),
                        V((32, 16, 128), BF), V((16, 16, 128), BF), V((16, 16, 128), BF),
                        V((256, 128), F32), V((256, 128), F32),
                        V((65, 64, 512), BF), V((33, 64, 512), BF), V((17, 64, 512), BF),
                        V((9, 64, 512), BF), V((4, 64, 512), BF), V((2, 64, 512), BF),
                        V((4, 4, 24, 128), F32), V((4, 64, 128), F32),
                        V((4, 3, 512, 512), BF), V((2, 2, 512, 512), BF), V((512, 1280), BF),
                        V((8, 80, 128), BF), V((3, 8, 80, 128), BF), V((3, 1552, 128), F32), V((3, 2, 2, 768, 256), BF),
                        V((256, 256), BF), V((2, 80, 80, 128), BF), V((10240, 128), F32), V((2, WROWS, 128), BF), V((2, 512, 128), F32),
                        V((2, 8, 64, 128), BF), V((2, 8, 64, 128), BF), V((256, 256), F32),
                        D((9,)), D((10,)), D((32,)), D((32,)), D((16,)), D((16,)), D((23,)), D((23,)), D((2, 7)), D((2, 7))],
        compiler_params=pltpu.CompilerParams(vmem_limit_bytes=VMEM_MB << 20, collective_id=0, has_side_effects=True),
        name="encoder",
    )(waveform, clip_lengths[:, :, 0], conv_first, conv_mid, conv_last, conv_gain, conv_shift, proj_gain[None], proj_shift[None],
      proj_weight, proj_bias.reshape(10, 128), jnp.transpose(pos_weight, (0, 2, 3, 1)), pos_bias.reshape(10, 128))


def solution(mesh):
    return jax.shard_map(
        per_device,
        mesh=mesh,
        in_specs=(P("fsdp", "dp", None),) + (P(),) * 10 + (P("fsdp", None, None, None), P()),
        out_specs=P("fsdp", "dp", None),
        check_vma=False,
    )
```
